32 devices in a mesh: gx: 8 (over z, x), gy: 4 (over y, core).
Axes of the slice: x: 2, y: 2, z: 4, core: 2. Of those that a mesh axis runs over, the one named last changes fastest.
Arguments:
- voxels: bfloat16 [64, 32, 8, 96], P('gx', 'gy'), may hold values from -6 to 6
- occupancy: int32 [64, 32, 8], P('gx', 'gy'), may hold values 0 or 1
- conv_weight: bfloat16 [27, 96, 96], replicated, may hold values from -0.125 to 0.125
- conv_bias: float32 [96], replicated, may hold values from -3 to 3
- down_weight: bfloat16 [27, 96, 96], replicated, may hold values from -0.125 to 0.125
- down_cotangent: bfloat16 [32, 16, 4, 96], P('gx', 'gy'), may hold values from -6 to 6
Outputs:
- down: bfloat16 [32, 16, 4, 96], P('gx', 'gy')
- grad_voxels: bfloat16 [64, 32, 8, 96], P('gx', 'gy')
- grad_conv: float32 [27, 96, 96], replicated
- grad_bias: float32 [96], replicated
- grad_down: float32 [27, 96, 96], replicated
The draws below stay inside these ranges and needn't reach their ends.
Inputs may be any that keep to these rules, and one draw needn't show every extreme that they name: `occupancy`: 0 or 1 for every voxel.
All inputs are finite; a program needn't handle non-finite values. No bound on the sum of `occupancy` on one device may be relied on, other than what follows from the above.
Results may differ from the reference program's by a relative error of at most 0.006.
Values may be sent and summed in bfloat16 or wider, within the bound.
No kernel may reach another device: no remote copies, remote signals or barrier semaphores. Data moves between devices by JAX's collectives and lax.ppermute only.
A program may use at most 64 MiB of HBM per device.

```python
import math
import jax
import jax.numpy as jnp
from jax import lax

C = 96
TAPS = 27
H = 8
NX = 64
NY = 32


def place_ends(entries, stream_key, least, high):
    spot = [jax.random.randint(jax.random.fold_in(stream_key, axis), (), 0, length) for axis, length in enumerate(entries.shape)]
    main_axis = entries.shape.index(max(entries.shape))
    neighbour = spot[:main_axis] + [(spot[main_axis] + 1) % entries.shape[main_axis]] + spot[main_axis + 1:]
    return entries.at[tuple(spot)].set(least).at[tuple(neighbour)].set(high)


def levels(rng, shape, split, low, top_value):
    def one(position, parts):
        draws = jax.random.uniform(jax.random.fold_in(jax.random.fold_in(rng, 6), position), (parts,), jnp.float32, low / len(split), top_value / len(split))
        return jnp.repeat(jnp.exp(draws), shape[position] // parts).reshape((-1,) + (1,) * (len(shape) - position - 1))

    factor_of = one(*split[0])
    for cut in split[1:]:
        factor_of = factor_of * one(*cut)
    return factor_of


def centred(own_key, dims, scale, limit, cuts=(), kind=jnp.bfloat16):
    array = scale * jax.random.normal(own_key, dims, jnp.float32)
    if cuts:
        array = array * levels(own_key, dims, cuts, -0.22, 0.18)
    return jnp.clip(array, -limit, limit).astype(kind)


def setup_inputs(seed: int = 0) -> dict:
    splits = jax.random.split(jax.random.key(seed), 7)
    return {
        "voxels": centred(splits[0], (NX, NY, H, C), 1.0, 6.0, ((0, 8), (1, 4))),
        "occupancy": place_ends((jax.random.randint(splits[1], (NX, NY, H), 0, 2) < 1).astype(jnp.int32), jax.random.fold_in(splits[1], 1), 0, 1),
        "conv_weight": centred(splits[2], (TAPS, C, C), (TAPS * C) ** -0.5, 0.125),
        "conv_bias": centred(splits[3], (C,), 0.5, 3.0, (), jnp.float32),
        "down_weight": centred(splits[4], (TAPS, C, C), (TAPS * C) ** -0.5, 0.125),
        "down_cotangent": centred(splits[5], (NX // 2, NY // 2, H // 2, C), 1.0, 6.0, ((0, 8), (1, 4))),
    }


TAP_OFFSETS = [(step_x, step_y, step_z) for step_x in (-1, 0, 1) for step_y in (-1, 0, 1) for step_z in (-1, 0, 1)]
PARITY_TERMS = {0: [(0, 0)], 1: [(1, 0), (-1, 1)]}

def conv_same(padded, weight, size_x, size_y, size_z):
    channels = padded.shape[-1]
    running = jnp.zeros((size_x * size_y * size_z, weight.shape[2]), jnp.float32)
    for tap_index, (step_x, step_y, step_z) in enumerate(TAP_OFFSETS):
        window = padded[1 + step_x:1 + step_x + size_x, 1 + step_y:1 + step_y + size_y, 1 + step_z:1 + step_z + size_z]
        running = running + jnp.dot(window.reshape(-1, channels), weight[tap_index], preferred_element_type=jnp.float32)
    return running.reshape(size_x, size_y, size_z, -1)

def weight_taps(padded, grad_out, size_x, size_y, size_z):
    channels = padded.shape[-1]
    flat_grad = grad_out.reshape(-1, grad_out.shape[-1])
    pieces = []
    for step_x, step_y, step_z in TAP_OFFSETS:
        window = padded[1 + step_x:1 + step_x + size_x, 1 + step_y:1 + step_y + size_y, 1 + step_z:1 + step_z + size_z]
        pieces.append(jnp.dot(window.reshape(-1, channels).T, flat_grad, preferred_element_type=jnp.float32))
    return jnp.stack(pieces)

def stride_window(padded, step_x, step_y, step_z, size_x, size_y, size_z):
    channels = padded.shape[-1]
    return lax.slice(padded, (1 + step_x, 1 + step_y, 1 + step_z, 0), (2 + step_x + 2 * (size_x - 1), 2 + step_y + 2 * (size_y - 1), 2 + step_z + 2 * (size_z - 1), channels), (2, 2, 2, 1))

def stride_conv(padded, weight, size_x, size_y, size_z):
    channels = padded.shape[-1]
    running = jnp.zeros((size_x * size_y * size_z, weight.shape[2]), jnp.float32)
    for tap_index, (step_x, step_y, step_z) in enumerate(TAP_OFFSETS):
        window = stride_window(padded, step_x, step_y, step_z, size_x, size_y, size_z)
        running = running + jnp.dot(window.reshape(-1, channels), weight[tap_index], preferred_element_type=jnp.float32)
    return running.reshape(size_x, size_y, size_z, -1)

def stride_weight(padded, grad_out, size_x, size_y, size_z):
    channels = padded.shape[-1]
    flat_grad = grad_out.reshape(-1, grad_out.shape[-1])
    pieces = []
    for step_x, step_y, step_z in TAP_OFFSETS:
        window = stride_window(padded, step_x, step_y, step_z, size_x, size_y, size_z)
        pieces.append(jnp.dot(window.reshape(-1, channels).T, flat_grad, preferred_element_type=jnp.float32))
    return jnp.stack(pieces)

def fine_from_coarse(padded, weight, size_x, size_y, size_z):
    channels = padded.shape[-1]
    flipped = jnp.swapaxes(weight, 1, 2)
    blocks = []
    for parity_x in (0, 1):
        for parity_y in (0, 1):
            for parity_z in (0, 1):
                running = jnp.zeros((size_x * size_y * size_z, weight.shape[1]), jnp.float32)
                for step_x, shift_x in PARITY_TERMS[parity_x]:
                    for step_y, shift_y in PARITY_TERMS[parity_y]:
                        for step_z, shift_z in PARITY_TERMS[parity_z]:
                            tap_index = (step_x + 1) * 9 + (step_y + 1) * 3 + (step_z + 1)
                            window = padded[shift_x:shift_x + size_x, shift_y:shift_y + size_y, shift_z:shift_z + size_z]
                            running = running + jnp.dot(window.reshape(-1, channels), flipped[tap_index], preferred_element_type=jnp.float32)
                blocks.append(running.reshape(size_x, size_y, size_z, -1))
    stacked = jnp.stack(blocks).reshape(2, 2, 2, size_x, size_y, size_z, -1)
    return jnp.transpose(stacked, (3, 0, 4, 1, 5, 2, 6)).reshape(2 * size_x, 2 * size_y, 2 * size_z, -1)

def reference(voxels, occupancy, conv_weight, conv_bias, down_weight, down_cotangent):
    size_x, size_y, size_z, channels = voxels.shape
    half_x, half_y, half_z = (size_x // 2, size_y // 2, size_z // 2)
    occupied = occupancy.astype(jnp.float32)[..., None]
    masked = (voxels.astype(jnp.float32) * occupied).astype(jnp.bfloat16)
    padded_in = jnp.pad(masked, ((1, 1), (1, 1), (1, 1), (0, 0)))
    preact = conv_same(padded_in, conv_weight, size_x, size_y, size_z) + conv_bias
    summed = (masked.astype(jnp.float32) + jax.nn.silu(preact) * occupied).astype(jnp.bfloat16)
    coarse_live = occupancy.reshape(half_x, 2, half_y, 2, half_z, 2).max(axis=(1, 3, 5)).astype(jnp.float32)[..., None]
    stride_in = jnp.pad(summed, ((1, 0), (1, 0), (1, 0), (0, 0)))
    down = (stride_conv(stride_in, down_weight, half_x, half_y, half_z) * coarse_live).astype(jnp.bfloat16)
    grad_coarse = (down_cotangent.astype(jnp.float32) * coarse_live).astype(jnp.bfloat16)
    grad_stride = stride_weight(stride_in, grad_coarse, half_x, half_y, half_z)
    coarse_pad = jnp.pad(grad_coarse, ((0, 1), (0, 1), (0, 1), (0, 0)))
    grad_sum = fine_from_coarse(coarse_pad, down_weight, half_x, half_y, half_z)
    sigmoid_val = jax.nn.sigmoid(preact)
    grad_pre = (grad_sum * occupied * sigmoid_val * (1.0 + preact * (1.0 - sigmoid_val))).astype(jnp.bfloat16)
    grad_bias = lax.optimization_barrier(jnp.sum(grad_pre.astype(jnp.float32), axis=(0, 1, 2)))
    grad_conv = weight_taps(padded_in, grad_pre, size_x, size_y, size_z)
    grad_padded = jnp.pad(grad_pre, ((1, 1), (1, 1), (1, 1), (0, 0)))
    back_weight = jnp.swapaxes(conv_weight[::-1], 1, 2)
    grad_in = grad_sum + conv_same(grad_padded, back_weight, size_x, size_y, size_z)
    grad_voxels = (grad_in * occupied).astype(jnp.bfloat16)
    factor = 1.0 / math.sqrt(size_x * size_y * size_z)
    return (down, grad_voxels, grad_conv * factor, grad_bias * factor, grad_stride * factor)
```

```python
import functools
import math

import jax
import jax.numpy as jnp
from jax import lax
from jax.experimental import pallas as pl
from jax.experimental.pallas import tpu as pltpu
from jax.sharding import Mesh
from jax.sharding import PartitionSpec as P

LANES = 128
F32 = jnp.float32
BF16 = jnp.bfloat16
NT = (((1,), (1,)), ((), ()))
TN = (((0,), (0,)), ((), ()))
VMEM_BYTES = 60 * 1024 * 1024


def call(body, outs, scratch=(), cost=None, name=None):
    return pl.pallas_call(
        body,
        out_shape=tuple(jax.ShapeDtypeStruct(s, d) for s, d in outs),
        scratch_shapes=[pltpu.VMEM(s, d) for s, d in scratch],
        compiler_params=pltpu.CompilerParams(vmem_limit_bytes=VMEM_BYTES),
        cost_estimate=cost,
        name=name,
    )


def lane_of(shape):
    return lax.broadcasted_iota(jnp.int32, shape, len(shape) - 1)


def z_of(shape):
    return lax.broadcasted_iota(jnp.int32, shape, len(shape) - 2)


def below(v):
    return jnp.where(z_of(v.shape) == 0, 0.0, pltpu.roll(v, 1, axis=1))


def above(v):
    top = v.shape[1] - 1
    return jnp.where(z_of(v.shape) == top, 0.0, pltpu.roll(v, top, axis=1))


def first_kernel(dims, vox_ref, occ_ref, cot_ref, x_ref, u_ref, core_ref, side_ref, xs, us):
    tx, ty, tz, ch = dims
    hx, hy = tx // 2, ty // 2
    occ = occ_ref[...].astype(F32).reshape(tx * ty, tz, LANES)
    xs[...] = jnp.zeros(xs.shape, F32)
    xs[:, :ch] = vox_ref[...].astype(F32)
    x = xs[...].reshape(tx * ty, tz, LANES)
    x = jnp.where(lane_of(x.shape) == ch, 1.0, x) * occ
    xs[...] = x.reshape(xs.shape)
    x_ref[...] = xs[...].astype(BF16)
    pairs = occ.reshape(hx, 2, hy, 2, tz, LANES)
    pairs = jnp.maximum(pairs[:, 0], pairs[:, 1])
    pairs = jnp.maximum(pairs[:, :, 0], pairs[:, :, 1]).reshape(hx * hy, tz, LANES)
    coarse = jnp.maximum(pairs, pltpu.roll(pairs, tz - 1, axis=1))
    us[...] = jnp.zeros(us.shape, F32)
    cot = jnp.concatenate(
        [cot_ref[...].astype(F32), jnp.zeros((hx * hy * tz // 2, LANES - ch), F32)], axis=1
    )
    us[pl.ds(0, hx * hy * tz // 2, stride=2), :] = cot
    u = us[...].reshape(hx * hy, tz, LANES)
    even = lax.rem(z_of(u.shape), 2) == 0
    u = jnp.where((lane_of(u.shape) == ch) & even, 1.0, u) * coarse
    us[...] = u.reshape(us.shape)
    u_ref[...] = us[...].astype(BF16)
    core = lax.axis_index("core")
    x4, u4 = xs.reshape(tx, ty, tz, LANES), us.reshape(hx, hy, tz, LANES)
    rows = tx * 2 * tz
    for ref, low in ((core_ref, core), (side_ref, 1 - core)):
        start = (1 - low) * (ty - 2)
        ref[:rows] = x4[:, pl.ds(start, 2)].reshape(rows, LANES).astype(BF16)
        ref[rows:] = (
            u4[:, pl.ds((1 - low) * (hy - 1), 1)].reshape(hx * tz, LANES).astype(BF16)
        )


def second_kernel(dims, x_ref, u_ref, core_ref, side_ref, near_ref, far_ref, xe, ue):
    tx, ty, tz, _ = dims
    widen(dims, x_ref, u_ref, core_ref, side_ref, xe, ue, 0, 0)
    odd = lax.rem(lax.axis_index("gx"), 2)
    rows = 2 * (ty + 4) * tz
    hx, hy = tx // 2, ty // 2
    for ref, low in ((near_ref, odd), (far_ref, 1 - odd)):
        ref[:rows] = xe[pl.ds((1 - low) * (tx - 2), 2)].reshape(rows, LANES).astype(BF16)
        ref[rows:] = (
            ue[pl.ds((1 - low) * (hx - 1), 1)].reshape((hy + 2) * tz, LANES).astype(BF16)
        )


def widen(dims, x_ref, u_ref, core_ref, side_ref, xe, ue, x0, u0):
    tx, ty, tz, _ = dims
    hx, hy = tx // 2, ty // 2
    rows = tx * 2 * tz
    core = lax.axis_index("core")
    xe[x0 : x0 + tx, 2 : 2 + ty] = x_ref[...].astype(F32).reshape(tx, ty, tz, LANES)
    ue[u0 : u0 + hx, 1 : 1 + hy] = u_ref[...].astype(F32).reshape(hx, hy, tz, LANES)
    for ref, low in ((core_ref, core), (side_ref, 1 - core)):
        xe[x0 : x0 + tx, pl.ds((1 - low) * (ty + 2), 2)] = (
            ref[:rows].astype(F32).reshape(tx, 2, tz, LANES)
        )
        ue[u0 : u0 + hx, pl.ds((1 - low) * (hy + 1), 1)] = (
            ref[rows:].astype(F32).reshape(hx, 1, tz, LANES)
        )


def pad_weight(ch, w_ref, out):
    out[...] = jnp.zeros(out.shape, BF16)
    for t in range(w_ref.shape[0]):
        out[t // 3, (t % 3) * LANES : (t % 3) * LANES + ch, :ch] = w_ref[t]


def transposed_taps(w, ab):
    return jnp.concatenate([w[ab, e * LANES : (e + 1) * LANES] for e in range(3)], axis=1)


def pack_block(block, ch):
    free = LANES - ch
    keep = ch * ch // LANES
    tail = block[keep:ch]
    parts = [
        pltpu.roll(tail, (LANES - free - p * free) % LANES, axis=1) for p in range(ch // free)
    ]
    parts = jnp.concatenate(parts, axis=0)
    main = block[:keep]
    return jnp.where(lane_of(main.shape) < ch, main, parts)


def unpack_block(packed, ch):
    free = LANES - ch
    keep = ch * ch // LANES
    tall = ch - keep
    lane = lane_of((tall, LANES))
    tail = None
    for p in range(ch // free):
        part = packed[p * tall : (p + 1) * tall]
        part = pltpu.roll(part, (free + p * free) % LANES, axis=1)
        tail = part if tail is None else jnp.where(lane < p * free, tail, part)
    return jnp.concatenate([packed, tail], axis=0)


def main_kernel(
    dims, half_rows, x_ref, u_ref, core_ref, side_ref, near_ref, far_ref, cw_ref, dw_ref, bias_ref,
    keep_ref, send_ref, gp_ref, gs_ref, s_ref,
    xe, ue, z3, u3, s3, acc, gsr, gp, wf, wd, pack,
):
    tx, ty, tz, ch = dims
    hx, hy = tx // 2, ty // 2
    ex, ey = tx + 2, ty + 2
    block_rows = ch * ch // LANES
    core = lax.axis_index("core")
    odd = lax.rem(lax.axis_index("gx"), 2)
    pad_weight(ch, cw_ref, wf)
    pad_weight(ch, dw_ref, wd)
    widen(dims, x_ref, u_ref, core_ref, side_ref, xe, ue, 2, 1)
    rows = 2 * (ty + 4) * tz
    for ref, low in ((near_ref, odd), (far_ref, 1 - odd)):
        xe[pl.ds((1 - low) * (tx + 2), 2)] = ref[:rows].astype(F32).reshape(2, ty + 4, tz, LANES)
        ue[pl.ds((1 - low) * (hx + 1), 1)] = ref[rows:].astype(F32).reshape(1, hy + 2, tz, LANES)

    def shift_x(i, _):
        v = xe[i]
        v = jnp.where(lane_of(v.shape) == ch + 1, 1.0, v)
        z3[i, :, :, :LANES] = below(v)
        z3[i, :, :, LANES : 2 * LANES] = v
        z3[i, :, :, 2 * LANES :] = above(v)
        return 0

    lax.fori_loop(0, tx + 4, shift_x, 0)
    for i in range(hx + 2):
        v = ue[i]
        u3[i, :, :, :LANES] = above(v)
        u3[i, :, :, LANES : 2 * LANES] = v
        u3[i, :, :, 2 * LANES :] = below(v)

    acc[...] = jnp.zeros(acc.shape, F32)

    def forward(ab, _):
        a, b = ab // 3, lax.rem(ab, 3)
        win = z3[pl.ds(a, ex), pl.ds(b, ey)].reshape(ex * ey * tz, 3 * LANES).astype(BF16)
        out = jnp.dot(win, wf[ab], preferred_element_type=F32)
        acc[...] += out.reshape(acc.shape)
        return 0

    lax.fori_loop(0, 9, forward, 0)

    terms = {0: ((2, 0), (0, 1)), 1: ((1, 1),)}
    for px in (0, 1):
        for py in (0, 1):
            total = None
            for a, sx in terms[px]:
                for b, sy in terms[py]:
                    win = u3[sx : sx + hx + 1, sy : sy + hy + 1]
                    win = win.reshape((hx + 1) * (hy + 1) * tz, 3 * LANES).astype(BF16)
                    out = lax.dot_general(
                        win, transposed_taps(wd, a * 3 + b), NT, preferred_element_type=F32
                    )
                    total = out if total is None else total + out
            gsr[:, px, :, py] = total.reshape(hx + 1, hy + 1, tz, LANES)

    def pointwise(i, _):
        v = acc[i] + bias_ref[...].reshape(1, 1, LANES)
        x = xe[i + 1, 1 : 1 + ey]
        live = jnp.broadcast_to(x[:, :, ch : ch + 1], x.shape)
        s = 1.0 / (1.0 + jnp.exp(-v))
        summed = (x + live * (v * s)).astype(BF16).astype(F32)
        for k, t in enumerate((below(summed), summed, above(summed))):
            s3[i // 2, lax.rem(i, 2), :, :, :, k * LANES : (k + 1) * LANES] = t.reshape(
                hy + 1, 2, tz, LANES
            )
        g = gsr[i // 2, lax.rem(i, 2)].reshape(ey, tz, LANES)
        gp[i] = (g * live * s * (1.0 + v * (1.0 - s))).astype(BF16).astype(F32)
        return 0

    lax.fori_loop(0, ex, pointwise, 0)

    pack[...] = jnp.zeros(pack.shape, F32)
    grad = gp[1 : 1 + tx, 1 : 1 + ty].reshape(tx * ty * tz, LANES).astype(BF16)

    def conv_taps(ab, _):
        a, b = ab // 3, lax.rem(ab, 3)
        win = z3[pl.ds(a + 1, tx), pl.ds(b + 1, ty)].reshape(tx * ty * tz, 3 * LANES).astype(BF16)
        out = lax.dot_general(win, grad, TN, preferred_element_type=F32)
        for e in range(3):
            at = pl.multiple_of((ab * 3 + e) * block_rows, 8)
            pack[0, pl.ds(at, block_rows)] = pack_block(out[e * LANES : e * LANES + ch], ch)

        @pl.when(ab == 4)
        def _():
            pack[0, 27 * block_rows : 27 * block_rows + 8] = out[LANES + ch : LANES + ch + 8]

        return 0

    lax.fori_loop(0, 9, conv_taps, 0)
    cot = u3[1 : 1 + hx, 1 : 1 + hy, :, LANES : 2 * LANES].reshape(hx * hy * tz, LANES).astype(BF16)

    def down_taps(ab, _):
        a, b = ab // 3, lax.rem(ab, 3)
        win = s3[pl.ds(a // 2, hx), lax.rem(a, 2), pl.ds(b // 2, hy), lax.rem(b, 2)]
        win = win.reshape(hx * hy * tz, 3 * LANES).astype(BF16)
        out = lax.dot_general(win, cot, TN, preferred_element_type=F32)
        for e in range(3):
            at = pl.multiple_of((ab * 3 + e) * block_rows, 8)
            pack[1, pl.ds(at, block_rows)] = pack_block(out[e * LANES : e * LANES + ch], ch)
        return 0

    lax.fori_loop(0, 9, down_taps, 0)
    keep_ref[...] = pack[core].astype(BF16)
    send_ref[...] = pack[1 - core].astype(BF16)
    gp_ref[...] = gp[...].reshape(ex * ey * tz, LANES).astype(BF16)
    gs_ref[...] = gsr[...].reshape(ex, ey, tz, LANES)[1 : 1 + tx, 1 : 1 + ty].reshape(
        tx * ty * tz, LANES
    )
    s_ref[...] = (
        s3[:, :, :, :, :, LANES : 2 * LANES].reshape(ex * ey * tz, LANES).astype(BF16)
    )


def second_outputs(
    dims, x_ref, u_ref, gp_ref, gs_ref, s_ref, cw_ref, dw_ref, down_ref, gv_ref,
    g3, s3, acc, accd, wf, wd,
):
    tx, ty, tz, ch = dims
    hx, hy = tx // 2, ty // 2
    ex, ey = tx + 2, ty + 2
    pad_weight(ch, cw_ref, wf)
    pad_weight(ch, dw_ref, wd)
    v = gp_ref[...].astype(F32).reshape(ex * ey, tz, LANES)
    for k, t in enumerate((above(v), v, below(v))):
        g3[:, :, :, k * LANES : (k + 1) * LANES] = t.reshape(ex, ey, tz, LANES)
    v = s_ref[...].astype(F32).reshape(ex * ey, tz, LANES)
    for k, t in enumerate((below(v), v, above(v))):
        s3[:, :, :, :, :, k * LANES : (k + 1) * LANES] = t.reshape(hx + 1, 2, hy + 1, 2, tz, LANES)
    acc[...] = gs_ref[...]
    accd[...] = jnp.zeros(accd.shape, F32)

    def taps(ab, _):
        a, b = ab // 3, lax.rem(ab, 3)
        win = g3[pl.ds(2 - a, tx), pl.ds(2 - b, ty)].reshape(tx * ty * tz, 3 * LANES).astype(BF16)
        acc[...] += lax.dot_general(win, transposed_taps(wf, ab), NT, preferred_element_type=F32)
        win = s3[pl.ds(a // 2, hx), lax.rem(a, 2), pl.ds(b // 2, hy), lax.rem(b, 2)]
        win = win.reshape(hx * hy * tz, 3 * LANES).astype(BF16)
        accd[...] += jnp.dot(win, wd[ab], preferred_element_type=F32)
        return 0

    lax.fori_loop(0, 9, taps, 0)
    x = x_ref[...].astype(F32)
    live = jnp.broadcast_to(x[:, ch : ch + 1], x.shape)
    gv_ref[...] = (acc[...] * live)[:, :ch].astype(BF16)
    u = u_ref[...].astype(F32)
    accd[...] = accd[...] * jnp.broadcast_to(u[:, ch : ch + 1], u.shape)
    down_ref[...] = accd[pl.ds(0, hx * hy * tz // 2, stride=2), :][:, :ch].astype(BF16)


def last_kernel(ch, factor, *refs):
    own, other = refs[:4], refs[4:8]
    conv_ref, down_ref, bias_ref, full = refs[8:]
    core = lax.axis_index("core")
    me = lax.rem(lax.axis_index("gx"), 2) * 2 + lax.rem(lax.axis_index("gyc"), 2)
    rows = own[0].shape[0]
    block_rows = ch * ch // LANES
    for k in range(4):
        at = pl.ds(pl.multiple_of((me ^ k) * rows, 16), rows)
        full[core, at] = own[k][...].astype(F32) * factor
        full[1 - core, at] = other[k][...].astype(F32) * factor
    for h, ref in ((0, conv_ref), (1, down_ref)):
        for t in range(27):
            block = unpack_block(full[h, t * block_rows : (t + 1) * block_rows], ch)
            ref[t] = block[:, :ch]
    bias_ref[...] = full[0, 27 * block_rows + 1 : 27 * block_rows + 2, :ch]


def on_device(voxels, occupancy, conv_weight, conv_bias, down_weight, down_cotangent):
    tx, ty, tz, ch = voxels.shape
    hx, hy, hz = tx // 2, ty // 2, tz // 2
    ex, ey = tx + 2, ty + 2
    dims = (tx, ty, tz, ch)
    n_gx, n_gyc = lax.axis_size("gx"), lax.axis_size("gyc")
    fine, coarse = tx * ty * tz, hx * hy * tz

    occ = jnp.broadcast_to(occupancy.astype(BF16)[..., None], (tx, ty, tz, LANES))
    side_rows = tx * 2 * tz + hx * tz
    row_rows = 2 * (ty + 4) * tz + (hy + 2) * tz
    x, u, to_core, to_side = call(
        functools.partial(first_kernel, dims),
        [((fine, LANES), BF16), ((coarse, LANES), BF16)] + [((side_rows, LANES), BF16)] * 2,
        [((fine, LANES), F32), ((coarse, LANES), F32)],
        name="first",
    )(
        voxels.reshape(fine, ch),
        occ.reshape(fine, LANES),
        down_cotangent.reshape(hx * hy * hz, ch),
    )
    swap = [(0, 1), (1, 0)]
    n_gy = n_gyc * 2
    sides = [(i, i + 1) for i in range(1, n_gy - 1, 2)]
    sides += [(j, i) for i, j in sides]
    from_core = lax.ppermute(to_core, "core", swap)
    from_side = lax.ppermute(to_side, ("gyc", "core"), sides)
    to_near, to_far = call(
        functools.partial(second_kernel, dims),
        [((row_rows, LANES), BF16)] * 2,
        [((tx, ty + 4, tz, LANES), F32), ((hx, hy + 2, tz, LANES), F32)],
        name="second",
    )(x, u, from_core, from_side)
    near = [(i, i ^ 1) for i in range(n_gx)]
    far = [(i, i + 1) for i in range(1, n_gx - 1, 2)]
    far += [(j, i) for i, j in far]
    from_near = lax.ppermute(to_near, "gx", near)
    from_far = lax.ppermute(to_far, "gx", far)

    block_rows = ch * ch // LANES
    half_rows = -(-(27 * block_rows + 8) // 64) * 64
    bias = jnp.pad(conv_bias, (0, LANES - ch)).reshape(1, LANES)
    keep, send, gp, gs, s = call(
        functools.partial(main_kernel, dims, half_rows),
        [((half_rows, LANES), BF16)] * 2
        + [((ex * ey * tz, LANES), BF16), ((fine, LANES), F32), ((ex * ey * tz, LANES), BF16)],
        [
            ((tx + 4, ty + 4, tz, LANES), F32),
            ((hx + 2, hy + 2, tz, LANES), F32),
            ((tx + 4, ty + 4, tz, 3 * LANES), F32),
            ((hx + 2, hy + 2, tz, 3 * LANES), F32),
            ((hx + 1, 2, hy + 1, 2, tz, 3 * LANES), F32),
            ((ex, ey, tz, LANES), F32),
            ((hx + 1, 2, hy + 1, 2, tz, LANES), F32),
            ((ex, ey, tz, LANES), F32),
            ((9, 3 * LANES, LANES), BF16),
            ((9, 3 * LANES, LANES), BF16),
            ((2, half_rows, LANES), F32),
        ],
        name="main",
    )(x, u, from_core, from_side, from_near, from_far, conv_weight, down_weight, bias)

    down, grad_voxels = call(
        functools.partial(second_outputs, dims),
        [((hx * hy * hz, ch), BF16), ((fine, ch), BF16)],
        [
            ((ex, ey, tz, 3 * LANES), F32),
            ((hx + 1, 2, hy + 1, 2, tz, 3 * LANES), F32),
            ((fine, LANES), F32),
            ((coarse, LANES), F32),
            ((9, 3 * LANES, LANES), BF16),
            ((9, 3 * LANES, LANES), BF16),
        ],
        cost=pl.CostEstimate(flops=5_000_000_000, bytes_accessed=4_000_000, transcendentals=0),
        name="outputs",
    )(x, u, gp, gs, s, conv_weight, down_weight)

    def plus(a, b):
        return (a.astype(F32) + b.astype(F32)).astype(BF16)

    got = lax.ppermute(send, "core", swap)
    me = lax.rem(lax.axis_index("gx"), 2) * 2 + lax.rem(lax.axis_index("gyc"), 2)
    quarter = half_rows // 4
    keep4, got4 = keep.reshape(4, quarter, LANES), got.reshape(4, quarter, LANES)

    def quarter_of(k):
        pick = functools.partial(lax.dynamic_index_in_dim, index=me ^ k, axis=0, keepdims=False)
        return pick(keep4).astype(F32) + pick(got4).astype(F32)

    def across(value, k):
        route = []
        for i in range(n_gx):
            for j in range(n_gyc):
                route.append((i * n_gyc + j, (i ^ (k >> 1)) * n_gyc + (j ^ (k & 1))))
        return lax.ppermute(value, ("gx", "gyc"), route)

    arrived = [across(quarter_of(k).astype(BF16), k) for k in (1, 2, 3)]
    total = quarter_of(0)
    for piece in arrived:
        total = total + piece.astype(F32)
    total = total.astype(BF16)
    for axis, peers in (("gx", n_gx), ("gyc", n_gyc)):
        step = 2
        while step < peers:
            total = plus(total, lax.ppermute(total, axis, [(i, i ^ step) for i in range(peers)]))
            step *= 2
    own = [total] + [across(total, k) for k in (1, 2, 3)]
    other = [lax.ppermute(piece, "core", swap) for piece in own]
    factor = 1.0 / math.sqrt(tx * n_gx * ty * n_gy * tz)
    grad_conv, grad_down, grad_bias = call(
        functools.partial(last_kernel, ch, factor),
        [((27, ch, ch), F32), ((27, ch, ch), F32), ((1, ch), F32)],
        [((2, half_rows, LANES), F32)],
        name="last",
    )(*own, *other)
    return (
        down.reshape(hx, hy, hz, ch),
        grad_voxels.reshape(tx, ty, tz, ch),
        grad_conv,
        grad_bias.reshape(ch),
        grad_down,
    )


def solution(mesh):
    n_gx, n_gy = mesh.shape["gx"], mesh.shape["gy"]
    split = Mesh(mesh.devices.reshape(n_gx, n_gy // 2, 2), ("gx", "gyc", "core"))
    gy = ("gyc", "core")
    placed = (
        P("gx", gy, None, None),
        P("gx", gy, None),
        P(),
        P(),
        P(),
        P("gx", gy, None, None),
    )
    return jax.shard_map(
        on_device,
        mesh=split,
        in_specs=placed,
        out_specs=(P("gx", gy, None, None), P("gx", gy, None, None), P(), P(), P()),
        check_vma=False,
    )
```

```python
import functools
import math

import jax
import jax.numpy as jnp
from jax import lax
from jax.experimental import pallas as pl
from jax.experimental.pallas import tpu as pltpu
from jax.sharding import Mesh
from jax.sharding import PartitionSpec as P

LANES = 128
F32 = jnp.float32
BF16 = jnp.bfloat16
NT = (((1,), (1,)), ((), ()))
TN = (((0,), (0,)), ((), ()))
MIB = 1024 * 1024


def call(body, outs, args, scratch=(), cost=None, name=None, vmem=8, in_hbm=False, sems=()):
    in_place = pl.BlockSpec(memory_space=pltpu.VMEM)
    placed = pl.BlockSpec(memory_space=pl.ANY) if in_hbm else in_place
    return pl.pallas_call(
        body,
        out_shape=tuple(jax.ShapeDtypeStruct(s, d) for s, d in outs),
        in_specs=[in_place] * len(args),
        out_specs=tuple(placed for _ in outs),
        scratch_shapes=[pltpu.VMEM(s, d) for s, d in scratch] + list(sems),
        compiler_params=pltpu.CompilerParams(vmem_limit_bytes=vmem * MIB),
        cost_estimate=cost,
        name=name,
    )(*args)


def lane_of(shape):
    return lax.broadcasted_iota(jnp.int32, shape, len(shape) - 1)


def z_of(shape):
    return lax.broadcasted_iota(jnp.int32, shape, len(shape) - 2)


def below(v):
    return jnp.where(z_of(v.shape) == 0, 0.0, pltpu.roll(v, 1, axis=1))


def above(v):
    top = v.shape[1] - 1
    return jnp.where(z_of(v.shape) == top, 0.0, pltpu.roll(v, top, axis=1))


def first_kernel(dims, vox_ref, occ_ref, cot_ref, x_ref, u_ref, core_ref, side_ref, xs, us):
    tx, ty, tz, ch = dims
    hx, hy = tx // 2, ty // 2
    occ = jnp.broadcast_to(occ_ref[...].astype(F32)[:, :, None], (tx * ty, tz, LANES))
    xs[...] = jnp.zeros(xs.shape, F32)
    xs[:, :ch] = vox_ref[...].astype(F32)
    x = xs[...].reshape(tx * ty, tz, LANES)
    x = jnp.where(lane_of(x.shape) == ch, 1.0, x) * occ
    xs[...] = x.reshape(xs.shape)
    x_ref[...] = xs[...].astype(BF16)
    pairs = occ.reshape(hx, 2, hy, 2, tz, LANES)
    pairs = jnp.maximum(pairs[:, 0], pairs[:, 1])
    pairs = jnp.maximum(pairs[:, :, 0], pairs[:, :, 1]).reshape(hx * hy, tz, LANES)
    coarse = jnp.maximum(pairs, pltpu.roll(pairs, tz - 1, axis=1))
    us[...] = jnp.zeros(us.shape, F32)
    cot = jnp.concatenate(
        [cot_ref[...].astype(F32), jnp.zeros((hx * hy * tz // 2, LANES - ch), F32)], axis=1
    )
    us[pl.ds(0, hx * hy * tz // 2, stride=2), :] = cot
    u = us[...].reshape(hx * hy, tz, LANES)
    even = lax.rem(z_of(u.shape), 2) == 0
    u = jnp.where((lane_of(u.shape) == ch) & even, 1.0, u) * coarse
    us[...] = u.reshape(us.shape)
    u_ref[...] = us[...].astype(BF16)
    core = lax.axis_index("core")
    x4, u4 = xs.reshape(tx, ty, tz, LANES), us.reshape(hx, hy, tz, LANES)
    rows = tx * 2 * tz
    for ref, low in ((core_ref, core), (side_ref, 1 - core)):
        start = (1 - low) * (ty - 2)
        ref[:rows] = x4[:, pl.ds(start, 2)].reshape(rows, LANES).astype(BF16)
        ref[rows:] = (
            u4[:, pl.ds((1 - low) * (hy - 1), 1)].reshape(hx * tz, LANES).astype(BF16)
        )


def second_kernel(dims, x_ref, u_ref, core_ref, side_ref, near_ref, far_ref, xe, ue):
    tx, ty, tz, _ = dims
    widen(dims, x_ref, u_ref, core_ref, side_ref, xe, ue, 0, 0)
    odd = lax.rem(lax.axis_index("gx"), 2)
    rows = 2 * (ty + 4) * tz
    hx, hy = tx // 2, ty // 2
    for ref, low in ((near_ref, odd), (far_ref, 1 - odd)):
        ref[:rows] = xe[pl.ds((1 - low) * (tx - 2), 2)].reshape(rows, LANES).astype(BF16)
        ref[rows:] = (
            ue[pl.ds((1 - low) * (hx - 1), 1)].reshape((hy + 2) * tz, LANES).astype(BF16)
        )


def widen(dims, x_ref, u_ref, core_ref, side_ref, xe, ue, x0, u0):
    tx, ty, tz, _ = dims
    hx, hy = tx // 2, ty // 2
    rows = tx * 2 * tz
    core = lax.axis_index("core")
    xe[x0 : x0 + tx, 2 : 2 + ty] = x_ref[...].astype(F32).reshape(tx, ty, tz, LANES)
    ue[u0 : u0 + hx, 1 : 1 + hy] = u_ref[...].astype(F32).reshape(hx, hy, tz, LANES)
    for ref, low in ((core_ref, core), (side_ref, 1 - core)):
        xe[x0 : x0 + tx, pl.ds((1 - low) * (ty + 2), 2)] = (
            ref[:rows].astype(F32).reshape(tx, 2, tz, LANES)
        )
        ue[u0 : u0 + hx, pl.ds((1 - low) * (hy + 1), 1)] = (
            ref[rows:].astype(F32).reshape(hx, 1, tz, LANES)
        )


def taps_in_rows(ch, w_ref, out):
    out[...] = jnp.zeros(out.shape, BF16)
    for t in range(w_ref.shape[0]):
        out[t // 3, (t % 3) * LANES : (t % 3) * LANES + ch, :ch] = w_ref[t]


def taps_in_lanes(ch, w_ref, out):
    out[...] = jnp.zeros(out.shape, BF16)
    for t in range(w_ref.shape[0]):
        at, lane = t // 3 * LANES, t % 3 * LANES
        out[at : at + ch, lane : lane + ch] = w_ref[t]


def three(v):
    return v[:, :, :LANES], v[:, :, LANES : 2 * LANES], v[:, :, 2 * LANES :]


def pack_block(block, ch):
    free = LANES - ch
    keep = ch * ch // LANES
    tail = block[keep:ch]
    parts = [
        pltpu.roll(tail, (LANES - free - p * free) % LANES, axis=1) for p in range(ch // free)
    ]
    parts = jnp.concatenate(parts, axis=0)
    main = block[:keep]
    return jnp.where(lane_of(main.shape) < ch, main, parts)


def unpack_block(packed, ch):
    free = LANES - ch
    keep = ch * ch // LANES
    tall = ch - keep
    lane = lane_of((tall, LANES))
    tail = None
    for p in range(ch // free):
        part = packed[p * tall : (p + 1) * tall]
        part = pltpu.roll(part, (free + p * free) % LANES, axis=1)
        tail = part if tail is None else jnp.where(lane < p * free, tail, part)
    return jnp.concatenate([packed, tail], axis=0)


def main_kernel(
    dims, x_ref, u_ref, core_ref, side_ref, near_ref, far_ref, cw_ref, dw_ref, bias_ref,
    keep_ref, send_ref, gp_ref, gs_ref, s_ref,
    xe, ue, ss, acc, gsr, gp, wf, wd, pack, bias,
):
    tx, ty, tz, ch = dims
    hx, hy = tx // 2, ty // 2
    ex, ey = tx + 2, ty + 2
    block_rows = ch * ch // LANES
    core = lax.axis_index("core")
    odd = lax.rem(lax.axis_index("gx"), 2)
    taps_in_lanes(ch, cw_ref, wf)
    taps_in_rows(ch, dw_ref, wd)
    bias[...] = jnp.zeros(bias.shape, F32)
    bias[:, :ch] = bias_ref[...]
    widen(dims, x_ref, u_ref, core_ref, side_ref, xe, ue, 2, 1)
    rows = 2 * (ty + 4) * tz
    for ref, low in ((near_ref, odd), (far_ref, 1 - odd)):
        xe[pl.ds((1 - low) * (tx + 2), 2)] = ref[:rows].astype(F32).reshape(2, ty + 4, tz, LANES)
        ue[pl.ds((1 - low) * (hx + 1), 1)] = ref[rows:].astype(F32).reshape(1, hy + 2, tz, LANES)

    part = ex // 2

    def forward(h, _):
        wins = [
            xe[pl.ds(h * part + a, part), b : b + ey].reshape(part * ey * tz, LANES).astype(BF16)
            for a in range(3)
            for b in range(3)
        ]
        out = jnp.dot(jnp.concatenate(wins, axis=1), wf[...], preferred_element_type=F32)
        lower, same, upper = three(out.reshape(part * ey, tz, 3 * LANES))
        out = below(lower) + same + above(upper)
        acc[pl.ds(h * part, part)] = out.reshape(part, ey, tz, LANES)
        return 0

    lax.fori_loop(0, 2, forward, 0)

    terms = {0: ((2, 0), (0, 1)), 1: ((1, 1),)}
    for px in (0, 1):
        for py in (0, 1):
            wins, taps = [], []
            for a, sx in terms[px]:
                for b, sy in terms[py]:
                    win = ue[sx : sx + hx + 1, sy : sy + hy + 1]
                    wins.append(win.reshape((hx + 1) * (hy + 1) * tz, LANES).astype(BF16))
                    taps.append(wd[a * 3 + b])
            out = lax.dot_general(
                jnp.concatenate(wins, axis=1), jnp.concatenate(taps, axis=1), NT,
                preferred_element_type=F32,
            )
            lower, same, upper = three(out.reshape((hx + 1) * (hy + 1), tz, 3 * LANES))
            out = above(lower) + same + below(upper)
            gsr[:, px, :, py] = out.reshape(hx + 1, hy + 1, tz, LANES)

    def pointwise(i, _):
        v = acc[i] + bias[...].reshape(1, 1, LANES)
        x = xe[i + 1, 1 : 1 + ey]
        live = jnp.broadcast_to(x[:, :, ch : ch + 1], x.shape)
        s = 1.0 / (1.0 + jnp.exp(-v))
        summed = (x + live * (v * s)).astype(BF16).astype(F32)
        ss[i // 2, lax.rem(i, 2)] = summed.reshape(hy + 1, 2, tz, LANES)
        g = gsr[i // 2, lax.rem(i, 2)].reshape(ey, tz, LANES)
        gp[i] = (g * live * s * (1.0 + v * (1.0 - s))).astype(BF16).astype(F32)
        return 0

    lax.fori_loop(0, ex, pointwise, 0)

    def gradients(h, wins, other):
        cells = other.shape[0] * other.shape[1]
        other = jnp.concatenate([above(other), other, below(other)], axis=2)
        other = other.reshape(cells, 3 * LANES).astype(BF16)
        for a in range(3):
            win = jnp.concatenate([wins(a, b) for b in range(3)], axis=1)
            out = lax.dot_general(win, other, TN, preferred_element_type=F32)
            for b in range(3):
                for e in range(3):
                    at = (a * 9 + b * 3 + e) * block_rows
                    block = out[b * LANES : b * LANES + ch, e * LANES : (e + 1) * LANES]
                    pack[h, at : at + block_rows] = pack_block(block, ch)
            if a == 1:
                at = 27 * block_rows
                pack[h, at : at + 8] = out[LANES + ch : LANES + ch + 8, LANES : 2 * LANES]
        at = 27 * block_rows + 8
        pack[h, at:] = jnp.zeros((pack.shape[1] - at, LANES), F32)

    def fine_window(a, b):
        win = xe[a + 1 : a + 1 + tx, b + 1 : b + 1 + ty]
        if a == 1 and b == 1:
            win = jnp.where(lane_of(win.shape) == ch + 1, 1.0, win)
        return win.reshape(tx * ty * tz, LANES).astype(BF16)

    def coarse_window(a, b):
        win = ss[a // 2 : a // 2 + hx, a % 2, b // 2 : b // 2 + hy, b % 2]
        return win.reshape(hx * hy * tz, LANES).astype(BF16)

    gradients(0, fine_window, gp[1 : 1 + tx, 1 : 1 + ty].reshape(tx * ty, tz, LANES))
    gradients(1, coarse_window, ue[1 : 1 + hx, 1 : 1 + hy].reshape(hx * hy, tz, LANES))
    keep_ref[...] = pack[core]
    send_ref[...] = pack[1 - core].astype(BF16)
    gp_ref[...] = gp[...].reshape(ex * ey * tz, LANES).astype(BF16)
    gs_ref[...] = gsr[...].reshape(ex, ey, tz, LANES)[1 : 1 + tx, 1 : 1 + ty].reshape(
        tx * ty * tz, LANES
    )
    s_ref[...] = ss[...].reshape(ex * ey * tz, LANES).astype(BF16)


def second_outputs(
    dims, x_ref, u_ref, gp_ref, gs_ref, s_ref, cw_ref, dw_ref, down_ref, gv_ref,
    ge, ss, accd, wf, wd,
):
    tx, ty, tz, ch = dims
    hx, hy = tx // 2, ty // 2
    ex, ey = tx + 2, ty + 2
    taps_in_rows(ch, cw_ref, wf)
    taps_in_lanes(ch, dw_ref, wd)
    ge[...] = gp_ref[...].astype(F32).reshape(ex, ey, tz, LANES)
    ss[...] = s_ref[...].astype(F32).reshape(hx + 1, 2, hy + 1, 2, tz, LANES)
    wins = [
        ss[a // 2 : a // 2 + hx, a % 2, b // 2 : b // 2 + hy, b % 2]
        .reshape(hx * hy * tz, LANES)
        .astype(BF16)
        for a in range(3)
        for b in range(3)
    ]
    out = jnp.dot(jnp.concatenate(wins, axis=1), wd[...], preferred_element_type=F32)
    lower, same, upper = three(out.reshape(hx * hy, tz, 3 * LANES))
    out = (below(lower) + same + above(upper)).reshape(hx * hy * tz, LANES)
    u = u_ref[...].astype(F32)
    accd[...] = out * jnp.broadcast_to(u[:, ch : ch + 1], u.shape)
    down_ref[...] = accd[pl.ds(0, hx * hy * tz // 2, stride=2), :][:, :ch].astype(BF16)

    wins = [
        ge[2 - a : 2 - a + tx, 2 - b : 2 - b + ty].reshape(tx * ty * tz, LANES).astype(BF16)
        for a in range(3)
        for b in range(3)
    ]
    taps = jnp.concatenate([wf[ab] for ab in range(9)], axis=1)
    out = lax.dot_general(
        jnp.concatenate(wins, axis=1), taps, NT, preferred_element_type=F32
    )
    lower, same, upper = three(out.reshape(tx * ty, tz, 3 * LANES))
    out = (above(lower) + same + below(upper)).reshape(tx * ty * tz, LANES)
    x = x_ref[...].astype(F32)
    live = jnp.broadcast_to(x[:, ch : ch + 1], x.shape)
    gv_ref[...] = ((gs_ref[...] + out) * live)[:, :ch].astype(BF16)


def last_kernel(ch, factor, *refs):
    own, other = refs[:4], refs[4:8]
    conv_ref, down_ref, bias_ref, full, conv_out, down_out, bias_out, sems = refs[8:]
    core = lax.axis_index("core")
    me = lax.rem(lax.axis_index("gx"), 2) * 2 + lax.rem(lax.axis_index("gyc"), 2)
    rows = own[0].shape[0]
    block_rows = ch * ch // LANES
    for k in range(4):
        at = pl.ds(pl.multiple_of((me ^ k) * rows, 16), rows)
        full[core, at] = own[k][...].astype(F32) * factor
        full[1 - core, at] = other[k][...].astype(F32) * factor
    bias_out[...] = full[0, 27 * block_rows + 1 : 27 * block_rows + 2, :ch]
    copies = [pltpu.make_async_copy(bias_out, bias_ref, sems.at[0])]
    copies[0].start()
    for h, ref, out in ((0, conv_ref, conv_out), (1, down_ref, down_out)):
        for a in range(3):
            for t in range(a * 9, a * 9 + 9):
                block = unpack_block(full[h, t * block_rows : (t + 1) * block_rows], ch)
                out[t] = block[:, :ch]
            part = pl.ds(a * 9, 9)
            copy = pltpu.make_async_copy(out.at[part], ref.at[part], sems.at[1 + h * 3 + a])
            copy.start()
            copies.append(copy)
    for copy in copies:
        copy.wait()


def on_device(voxels, occupancy, conv_weight, conv_bias, down_weight, down_cotangent):
    tx, ty, tz, ch = voxels.shape
    hx, hy, hz = tx // 2, ty // 2, tz // 2
    ex, ey = tx + 2, ty + 2
    dims = (tx, ty, tz, ch)
    n_gx, n_gyc = lax.axis_size("gx"), lax.axis_size("gyc")
    fine, coarse = tx * ty * tz, hx * hy * tz

    side_rows = tx * 2 * tz + hx * tz
    row_rows = 2 * (ty + 4) * tz + (hy + 2) * tz
    x, u, to_core, to_side = call(
        functools.partial(first_kernel, dims),
        [((fine, LANES), BF16), ((coarse, LANES), BF16)] + [((side_rows, LANES), BF16)] * 2,
        (
            voxels.reshape(fine, ch),
            occupancy.reshape(tx * ty, tz),
            down_cotangent.reshape(hx * hy * hz, ch),
        ),
        [((fine, LANES), F32), ((coarse, LANES), F32)],
        name="first",
        vmem=4,
    )
    swap = [(0, 1), (1, 0)]
    n_gy = n_gyc * 2
    sides = [(i, i + 1) for i in range(1, n_gy - 1, 2)]
    sides += [(j, i) for i, j in sides]
    from_core = lax.ppermute(to_core, "core", swap)
    from_side = lax.ppermute(to_side, ("gyc", "core"), sides)
    to_near, to_far = call(
        functools.partial(second_kernel, dims),
        [((row_rows, LANES), BF16)] * 2,
        (x, u, from_core, from_side),
        [((tx, ty + 4, tz, LANES), F32), ((hx, hy + 2, tz, LANES), F32)],
        name="second",
        vmem=4,
    )
    near = [(i, i ^ 1) for i in range(n_gx)]
    far = [(i, i + 1) for i in range(1, n_gx - 1, 2)]
    far += [(j, i) for i, j in far]
    from_near = lax.ppermute(to_near, "gx", near)
    from_far = lax.ppermute(to_far, "gx", far)

    block_rows = ch * ch // LANES
    half_rows = -(-(27 * block_rows + 8) // 64) * 64
    keep, send, gp, gs, s = call(
        functools.partial(main_kernel, dims),
        [((half_rows, LANES), F32), ((half_rows, LANES), BF16)]
        + [((ex * ey * tz, LANES), BF16), ((fine, LANES), F32), ((ex * ey * tz, LANES), BF16)],
        (
            x, u, from_core, from_side, from_near, from_far, conv_weight, down_weight,
            conv_bias.reshape(1, ch),
        ),
        [
            ((tx + 4, ty + 4, tz, LANES), F32),
            ((hx + 2, hy + 2, tz, LANES), F32),
            ((hx + 1, 2, hy + 1, 2, tz, LANES), F32),
            ((ex, ey, tz, LANES), F32),
            ((hx + 1, 2, hy + 1, 2, tz, LANES), F32),
            ((ex, ey, tz, LANES), F32),
            ((9 * LANES, 3 * LANES), BF16),
            ((9, 3 * LANES, LANES), BF16),
            ((2, half_rows, LANES), F32),
            ((1, LANES), F32),
        ],
        name="main",
        vmem=24,
    )

    down, grad_voxels = call(
        functools.partial(second_outputs, dims),
        [((hx * hy * hz, ch), BF16), ((fine, ch), BF16)],
        (x, u, gp, gs, s, conv_weight, down_weight),
        [
            ((ex, ey, tz, LANES), F32),
            ((hx + 1, 2, hy + 1, 2, tz, LANES), F32),
            ((coarse, LANES), F32),
            ((9, 3 * LANES, LANES), BF16),
            ((9 * LANES, 3 * LANES), BF16),
        ],
        cost=pl.CostEstimate(flops=5_000_000_000, bytes_accessed=4_000_000, transcendentals=0),
        name="outputs",
        vmem=24,
    )

    def plus(a, b):
        return (a.astype(F32) + b.astype(F32)).astype(BF16)

    got = lax.ppermute(send, "core", swap)
    me = lax.rem(lax.axis_index("gx"), 2) * 2 + lax.rem(lax.axis_index("gyc"), 2)
    quarter = half_rows // 4
    keep4, got4 = keep.reshape(4, quarter, LANES), got.reshape(4, quarter, LANES)

    def quarter_of(k):
        pick = functools.partial(lax.dynamic_index_in_dim, index=me ^ k, axis=0, keepdims=False)
        return pick(keep4).astype(F32) + pick(got4).astype(F32)

    def across(value, k):
        route = []
        for i in range(n_gx):
            for j in range(n_gyc):
                route.append((i * n_gyc + j, (i ^ (k >> 1)) * n_gyc + (j ^ (k & 1))))
        return lax.ppermute(value, ("gx", "gyc"), route)

    arrived = [across(quarter_of(k).astype(BF16), k) for k in (1, 2, 3)]
    *arrived, down, grad_voxels = lax.optimization_barrier((*arrived, down, grad_voxels))
    total = quarter_of(0)
    for piece in arrived:
        total = total + piece.astype(F32)
    total = total.astype(BF16)
    for axis, peers in (("gx", n_gx), ("gyc", n_gyc)):
        step = 2
        while step < peers:
            total = plus(total, lax.ppermute(total, axis, [(i, i ^ step) for i in range(peers)]))
            step *= 2
    own = [total] + [across(total, k) for k in (1, 2, 3)]
    other = [lax.ppermute(piece, "core", swap) for piece in own]
    factor = 1.0 / math.sqrt(tx * n_gx * ty * n_gy * tz)
    grad_conv, grad_down, grad_bias = call(
        functools.partial(last_kernel, ch, factor),
        [((27, ch, ch), F32), ((27, ch, ch), F32), ((1, ch), F32)],
        (*own, *other),
        [
            ((2, half_rows, LANES), F32),
            ((27, ch, ch), F32),
            ((27, ch, ch), F32),
            ((1, ch), F32),
        ],
        name="last",
        vmem=12,
        in_hbm=True,
        sems=[pltpu.SemaphoreType.DMA((7,))],
    )
    return (
        down.reshape(hx, hy, hz, ch),
        grad_voxels.reshape(tx, ty, tz, ch),
        grad_conv,
        grad_bias.reshape(ch),
        grad_down,
    )


def solution(mesh):
    n_gx, n_gy = mesh.shape["gx"], mesh.shape["gy"]
    split = Mesh(mesh.devices.reshape(n_gx, n_gy // 2, 2), ("gx", "gyc", "core"))
    gy = ("gyc", "core")
    placed = (
        P("gx", gy, None, None),
        P("gx", gy, None),
        P(),
        P(),
        P(),
        P("gx", gy, None, None),
    )
    return jax.shard_map(
        on_device,
        mesh=split,
        in_specs=placed,
        out_specs=(P("gx", gy, None, None), P("gx", gy, None, None), P(), P(), P()),
        check_vma=False,
    )
```

```python
import functools
import math

import jax
import jax.numpy as jnp
from jax import lax
from jax.experimental import pallas as pl
from jax.experimental.pallas import tpu as pltpu
from jax.sharding import Mesh
from jax.sharding import PartitionSpec as P

LANES = 128
F32 = jnp.float32
BF16 = jnp.bfloat16
NT = (((1,), (1,)), ((), ()))
TN = (((0,), (0,)), ((), ()))
MIB = 1024 * 1024


def call(body, outs, args, scratch=(), cost=None, name=None, vmem=8, far=(), far_outs=False, sems=0):
    near_spec = pl.BlockSpec(memory_space=pltpu.VMEM)
    far_spec = pl.BlockSpec(memory_space=pltpu.HBM)
    args = [
        pltpu.with_memory_space_constraint(a, pltpu.HBM) if i in far else a
        for i, a in enumerate(args)
    ]
    return pl.pallas_call(
        body,
        out_shape=tuple(jax.ShapeDtypeStruct(s, d) for s, d in outs),
        in_specs=[far_spec if i in far else near_spec for i in range(len(args))],
        out_specs=tuple(far_spec if far_outs else near_spec for _ in outs),
        scratch_shapes=[pltpu.VMEM(s, d) for s, d in scratch]
        + ([pltpu.SemaphoreType.DMA((sems,))] if sems else []),
        compiler_params=pltpu.CompilerParams(vmem_limit_bytes=vmem * MIB),
        cost_estimate=cost,
        name=name,
    )(*args)


def fetch(pairs, sems):
    copies = [pltpu.make_async_copy(a, b, sems.at[i]) for i, (a, b) in enumerate(pairs)]
    for copy in copies:
        copy.start()
    for copy in copies:
        copy.wait()


def lane_of(shape):
    return lax.broadcasted_iota(jnp.int32, shape, len(shape) - 1)


def z_of(shape):
    return lax.broadcasted_iota(jnp.int32, shape, len(shape) - 2)


def below(v):
    return jnp.where(z_of(v.shape) == 0, 0.0, pltpu.roll(v, 1, axis=1))


def above(v):
    top = v.shape[1] - 1
    return jnp.where(z_of(v.shape) == top, 0.0, pltpu.roll(v, top, axis=1))


def first_kernel(
    dims, vox_far, occ_far, cot_far, x_ref, u_ref, core_ref, side_ref,
    xs, us, vox_ref, occ_ref, cot_ref, sems,
):
    tx, ty, tz, ch = dims
    fetch(((vox_far, vox_ref), (occ_far, occ_ref), (cot_far, cot_ref)), sems)
    hx, hy = tx // 2, ty // 2
    occ = jnp.broadcast_to(occ_ref[...].astype(F32)[:, :, None], (tx * ty, tz, LANES))
    xs[...] = jnp.zeros(xs.shape, F32)
    xs[:, :ch] = vox_ref[...].astype(F32)
    x = xs[...].reshape(tx * ty, tz, LANES)
    x = jnp.where(lane_of(x.shape) == ch, 1.0, x) * occ
    xs[...] = x.reshape(xs.shape)
    x_ref[...] = xs[...].astype(BF16)
    pairs = occ.reshape(hx, 2, hy, 2, tz, LANES)
    pairs = jnp.maximum(pairs[:, 0], pairs[:, 1])
    pairs = jnp.maximum(pairs[:, :, 0], pairs[:, :, 1]).reshape(hx * hy, tz, LANES)
    coarse = jnp.maximum(pairs, pltpu.roll(pairs, tz - 1, axis=1))
    us[...] = jnp.zeros(us.shape, F32)
    cot = jnp.concatenate(
        [cot_ref[...].astype(F32), jnp.zeros((hx * hy * tz // 2, LANES - ch), F32)], axis=1
    )
    us[pl.ds(0, hx * hy * tz // 2, stride=2), :] = cot
    u = us[...].reshape(hx * hy, tz, LANES)
    even = lax.rem(z_of(u.shape), 2) == 0
    u = jnp.where((lane_of(u.shape) == ch) & even, 1.0, u) * coarse
    us[...] = u.reshape(us.shape)
    u_ref[...] = us[...].astype(BF16)
    core = lax.axis_index("core")
    x4, u4 = xs.reshape(tx, ty, tz, LANES), us.reshape(hx, hy, tz, LANES)
    rows = tx * 2 * tz
    for ref, low in ((core_ref, core), (side_ref, 1 - core)):
        start = (1 - low) * (ty - 2)
        ref[:rows] = x4[:, pl.ds(start, 2)].reshape(rows, LANES).astype(BF16)
        ref[rows:] = (
            u4[:, pl.ds((1 - low) * (hy - 1), 1)].reshape(hx * tz, LANES).astype(BF16)
        )


def second_kernel(dims, x_ref, u_ref, core_ref, side_ref, near_ref, far_ref, xe, ue):
    tx, ty, tz, _ = dims
    widen(dims, x_ref, u_ref, core_ref, side_ref, xe, ue, 0, 0)
    odd = lax.rem(lax.axis_index("gx"), 2)
    rows = 2 * (ty + 4) * tz
    hx, hy = tx // 2, ty // 2
    for ref, low in ((near_ref, odd), (far_ref, 1 - odd)):
        ref[:rows] = xe[pl.ds((1 - low) * (tx - 2), 2)].reshape(rows, LANES).astype(BF16)
        ref[rows:] = (
            ue[pl.ds((1 - low) * (hx - 1), 1)].reshape((hy + 2) * tz, LANES).astype(BF16)
        )


def widen(dims, x_ref, u_ref, core_ref, side_ref, xe, ue, x0, u0):
    tx, ty, tz, _ = dims
    hx, hy = tx // 2, ty // 2
    rows = tx * 2 * tz
    core = lax.axis_index("core")
    xe[x0 : x0 + tx, 2 : 2 + ty] = x_ref[...].astype(F32).reshape(tx, ty, tz, LANES)
    ue[u0 : u0 + hx, 1 : 1 + hy] = u_ref[...].astype(F32).reshape(hx, hy, tz, LANES)
    for ref, low in ((core_ref, core), (side_ref, 1 - core)):
        xe[x0 : x0 + tx, pl.ds((1 - low) * (ty + 2), 2)] = (
            ref[:rows].astype(F32).reshape(tx, 2, tz, LANES)
        )
        ue[u0 : u0 + hx, pl.ds((1 - low) * (hy + 1), 1)] = (
            ref[rows:].astype(F32).reshape(hx, 1, tz, LANES)
        )


def taps_in_rows(ch, w_ref, out):
    out[...] = jnp.zeros(out.shape, BF16)
    for t in range(w_ref.shape[0]):
        out[t // 3, (t % 3) * LANES : (t % 3) * LANES + ch, :ch] = w_ref[t]


def taps_in_lanes(ch, w_ref, out):
    out[...] = jnp.zeros(out.shape, BF16)
    for t in range(w_ref.shape[0]):
        at, lane = t // 3 * LANES, t % 3 * LANES
        out[at : at + ch, lane : lane + ch] = w_ref[t]


def weights_kernel(ch, cw_far, dw_far, bias_far, cl_ref, dr_ref, b_ref, cw, dw, bias, sems):
    fetch(((cw_far, cw), (dw_far, dw), (bias_far, bias)), sems)
    taps_in_lanes(ch, cw, cl_ref)
    taps_in_rows(ch, dw, dr_ref)
    b_ref[...] = jnp.zeros(b_ref.shape, F32)
    b_ref[:, :ch] = bias[...]


def other_weights_kernel(ch, cw, dw, cr_ref, dl_ref):
    taps_in_rows(ch, cw, cr_ref)
    taps_in_lanes(ch, dw, dl_ref)


def three(v):
    return v[:, :, :LANES], v[:, :, LANES : 2 * LANES], v[:, :, 2 * LANES :]


def pack_block(block, ch):
    free = LANES - ch
    keep = ch * ch // LANES
    tail = block[keep:ch]
    parts = [
        pltpu.roll(tail, (LANES - free - p * free) % LANES, axis=1) for p in range(ch // free)
    ]
    parts = jnp.concatenate(parts, axis=0)
    main = block[:keep]
    return jnp.where(lane_of(main.shape) < ch, main, parts)


def unpack_block(packed, ch):
    free = LANES - ch
    keep = ch * ch // LANES
    tall = ch - keep
    lane = lane_of((tall, LANES))
    tail = None
    for p in range(ch // free):
        part = packed[p * tall : (p + 1) * tall]
        part = pltpu.roll(part, (free + p * free) % LANES, axis=1)
        tail = part if tail is None else jnp.where(lane < p * free, tail, part)
    return jnp.concatenate([packed, tail], axis=0)


def main_kernel(
    dims, x_ref, u_ref, core_ref, side_ref, near_ref, far_ref, wf, wd, bias,
    keep_ref, send_ref, gp_ref, gs_ref, s_ref,
    xe, ue, ss, acc, gsr, gp, pack,
):
    tx, ty, tz, ch = dims
    hx, hy = tx // 2, ty // 2
    ex, ey = tx + 2, ty + 2
    block_rows = ch * ch // LANES
    core = lax.axis_index("core")
    odd = lax.rem(lax.axis_index("gx"), 2)
    widen(dims, x_ref, u_ref, core_ref, side_ref, xe, ue, 2, 1)
    rows = 2 * (ty + 4) * tz
    for ref, low in ((near_ref, odd), (far_ref, 1 - odd)):
        xe[pl.ds((1 - low) * (tx + 2), 2)] = ref[:rows].astype(F32).reshape(2, ty + 4, tz, LANES)
        ue[pl.ds((1 - low) * (hx + 1), 1)] = ref[rows:].astype(F32).reshape(1, hy + 2, tz, LANES)

    part = ex // 2

    def forward(h, _):
        wins = [
            xe[pl.ds(h * part + a, part), b : b + ey].reshape(part * ey * tz, LANES).astype(BF16)
            for a in range(3)
            for b in range(3)
        ]
        out = jnp.dot(jnp.concatenate(wins, axis=1), wf[...], preferred_element_type=F32)
        lower, same, upper = three(out.reshape(part * ey, tz, 3 * LANES))
        out = below(lower) + same + above(upper)
        acc[pl.ds(h * part, part)] = out.reshape(part, ey, tz, LANES)
        return 0

    lax.fori_loop(0, 2, forward, 0)

    terms = {0: ((2, 0), (0, 1)), 1: ((1, 1),)}
    for px in (0, 1):
        for py in (0, 1):
            wins, taps = [], []
            for a, sx in terms[px]:
                for b, sy in terms[py]:
                    win = ue[sx : sx + hx + 1, sy : sy + hy + 1]
                    wins.append(win.reshape((hx + 1) * (hy + 1) * tz, LANES).astype(BF16))
                    taps.append(wd[a * 3 + b])
            out = lax.dot_general(
                jnp.concatenate(wins, axis=1), jnp.concatenate(taps, axis=1), NT,
                preferred_element_type=F32,
            )
            lower, same, upper = three(out.reshape((hx + 1) * (hy + 1), tz, 3 * LANES))
            out = above(lower) + same + below(upper)
            gsr[:, px, :, py] = out.reshape(hx + 1, hy + 1, tz, LANES)

    def pointwise(i, _):
        v = acc[i] + bias[...].reshape(1, 1, LANES)
        x = xe[i + 1, 1 : 1 + ey]
        live = jnp.broadcast_to(x[:, :, ch : ch + 1], x.shape)
        s = 1.0 / (1.0 + jnp.exp(-v))
        summed = (x + live * (v * s)).astype(BF16).astype(F32)
        ss[i // 2, lax.rem(i, 2)] = summed.reshape(hy + 1, 2, tz, LANES)
        g = gsr[i // 2, lax.rem(i, 2)].reshape(ey, tz, LANES)
        gp[i] = (g * live * s * (1.0 + v * (1.0 - s))).astype(BF16).astype(F32)
        return 0

    lax.fori_loop(0, ex, pointwise, 0)

    def gradients(h, wins, other):
        cells = other.shape[0] * other.shape[1]
        other = jnp.concatenate([above(other), other, below(other)], axis=2)
        other = other.reshape(cells, 3 * LANES).astype(BF16)
        for a in range(3):
            win = jnp.concatenate([wins(a, b) for b in range(3)], axis=1)
            out = lax.dot_general(win, other, TN, preferred_element_type=F32)
            for b in range(3):
                for e in range(3):
                    at = (a * 9 + b * 3 + e) * block_rows
                    block = out[b * LANES : b * LANES + ch, e * LANES : (e + 1) * LANES]
                    pack[h, at : at + block_rows] = pack_block(block, ch)
            if a == 1:
                at = 27 * block_rows
                pack[h, at : at + 8] = out[LANES + ch : LANES + ch + 8, LANES : 2 * LANES]
        at = 27 * block_rows + 8
        pack[h, at:] = jnp.zeros((pack.shape[1] - at, LANES), F32)

    def fine_window(a, b):
        win = xe[a + 1 : a + 1 + tx, b + 1 : b + 1 + ty]
        if a == 1 and b == 1:
            win = jnp.where(lane_of(win.shape) == ch + 1, 1.0, win)
        return win.reshape(tx * ty * tz, LANES).astype(BF16)

    def coarse_window(a, b):
        win = ss[a // 2 : a // 2 + hx, a % 2, b // 2 : b // 2 + hy, b % 2]
        return win.reshape(hx * hy * tz, LANES).astype(BF16)

    gradients(0, fine_window, gp[1 : 1 + tx, 1 : 1 + ty].reshape(tx * ty, tz, LANES))
    gradients(1, coarse_window, ue[1 : 1 + hx, 1 : 1 + hy].reshape(hx * hy, tz, LANES))
    keep_ref[...] = pack[core]
    send_ref[...] = pack[1 - core].astype(BF16)
    gp_ref[...] = gp[...].reshape(ex * ey * tz, LANES).astype(BF16)
    gs_ref[...] = gsr[...].reshape(ex, ey, tz, LANES)[1 : 1 + tx, 1 : 1 + ty].reshape(
        tx * ty * tz, LANES
    )
    s_ref[...] = ss[...].reshape(ex * ey * tz, LANES).astype(BF16)


def second_outputs(
    dims, x_ref, u_ref, gp_ref, gs_ref, s_ref, wf, wd, down_ref, gv_ref,
    ge, ss, accd,
):
    tx, ty, tz, ch = dims
    hx, hy = tx // 2, ty // 2
    ex, ey = tx + 2, ty + 2
    ge[...] = gp_ref[...].astype(F32).reshape(ex, ey, tz, LANES)
    ss[...] = s_ref[...].astype(F32).reshape(hx + 1, 2, hy + 1, 2, tz, LANES)
    wins = [
        ss[a // 2 : a // 2 + hx, a % 2, b // 2 : b // 2 + hy, b % 2]
        .reshape(hx * hy * tz, LANES)
        .astype(BF16)
        for a in range(3)
        for b in range(3)
    ]
    out = jnp.dot(jnp.concatenate(wins, axis=1), wd[...], preferred_element_type=F32)
    lower, same, upper = three(out.reshape(hx * hy, tz, 3 * LANES))
    out = (below(lower) + same + above(upper)).reshape(hx * hy * tz, LANES)
    u = u_ref[...].astype(F32)
    accd[...] = out * jnp.broadcast_to(u[:, ch : ch + 1], u.shape)
    down_ref[...] = accd[pl.ds(0, hx * hy * tz // 2, stride=2), :][:, :ch].astype(BF16)

    wins = [
        ge[2 - a : 2 - a + tx, 2 - b : 2 - b + ty].reshape(tx * ty * tz, LANES).astype(BF16)
        for a in range(3)
        for b in range(3)
    ]
    taps = jnp.concatenate([wf[ab] for ab in range(9)], axis=1)
    out = lax.dot_general(
        jnp.concatenate(wins, axis=1), taps, NT, preferred_element_type=F32
    )
    lower, same, upper = three(out.reshape(tx * ty, tz, 3 * LANES))
    out = (above(lower) + same + below(upper)).reshape(tx * ty * tz, LANES)
    x = x_ref[...].astype(F32)
    live = jnp.broadcast_to(x[:, ch : ch + 1], x.shape)
    gv_ref[...] = ((gs_ref[...] + out) * live)[:, :ch].astype(BF16)


def split_kernel(keep_ref, got_ref, own_ref, *to_refs):
    me = lax.rem(lax.axis_index("gx"), 2) * 2 + lax.rem(lax.axis_index("gyc"), 2)
    rows = own_ref.shape[0]
    for k, ref in enumerate((own_ref, *to_refs)):
        at = pl.ds(pl.multiple_of((me ^ k) * rows, 16), rows)
        ref[...] = (keep_ref[at] + got_ref[at].astype(F32)).astype(ref.dtype)


def sum_kernel(own_ref, a_ref, b_ref, c_ref, out_ref):
    out_ref[...] = (
        own_ref[...] + a_ref[...].astype(F32) + b_ref[...].astype(F32) + c_ref[...].astype(F32)
    ).astype(BF16)


def last_kernel(ch, factor, *refs):
    own, other = refs[:4], refs[4:8]
    conv_ref, down_ref, bias_ref, full, conv_out, down_out, bias_out, sems = refs[8:]
    core = lax.axis_index("core")
    me = lax.rem(lax.axis_index("gx"), 2) * 2 + lax.rem(lax.axis_index("gyc"), 2)
    rows = own[0].shape[0]
    block_rows = ch * ch // LANES
    for k in range(4):
        at = pl.ds(pl.multiple_of((me ^ k) * rows, 16), rows)
        full[core, at] = own[k][...].astype(F32) * factor
        full[1 - core, at] = other[k][...].astype(F32) * factor
    bias_out[...] = full[0, 27 * block_rows + 1 : 27 * block_rows + 2, :ch]
    copies = [pltpu.make_async_copy(bias_out, bias_ref, sems.at[0])]
    copies[0].start()
    for h, ref, out in ((0, conv_ref, conv_out), (1, down_ref, down_out)):
        for a in range(3):
            for t in range(a * 9, a * 9 + 9):
                block = unpack_block(full[h, t * block_rows : (t + 1) * block_rows], ch)
                out[t] = block[:, :ch]
            part = pl.ds(a * 9, 9)
            copy = pltpu.make_async_copy(out.at[part], ref.at[part], sems.at[1 + h * 3 + a])
            copy.start()
            copies.append(copy)
    for copy in copies:
        copy.wait()


def on_device(voxels, occupancy, conv_weight, conv_bias, down_weight, down_cotangent):
    tx, ty, tz, ch = voxels.shape
    hx, hy, hz = tx // 2, ty // 2, tz // 2
    ex, ey = tx + 2, ty + 2
    dims = (tx, ty, tz, ch)
    n_gx, n_gyc = lax.axis_size("gx"), lax.axis_size("gyc")
    fine, coarse = tx * ty * tz, hx * hy * tz

    side_rows = tx * 2 * tz + hx * tz
    row_rows = 2 * (ty + 4) * tz + (hy + 2) * tz
    x, u, to_core, to_side = call(
        functools.partial(first_kernel, dims),
        [((fine, LANES), BF16), ((coarse, LANES), BF16)] + [((side_rows, LANES), BF16)] * 2,
        (
            voxels.reshape(fine, ch),
            occupancy.reshape(tx * ty, tz),
            down_cotangent.reshape(hx * hy * hz, ch),
        ),
        [
            ((fine, LANES), F32),
            ((coarse, LANES), F32),
            ((fine, ch), BF16),
            ((tx * ty, tz), jnp.int32),
            ((hx * hy * hz, ch), BF16),
        ],
        name="first",
        vmem=4,
        far=(0, 1, 2),
        sems=3,
    )
    swap = [(0, 1), (1, 0)]
    n_gy = n_gyc * 2
    sides = [(i, i + 1) for i in range(1, n_gy - 1, 2)]
    sides += [(j, i) for i, j in sides]
    from_core = lax.ppermute(to_core, "core", swap)
    from_side = lax.ppermute(to_side, ("gyc", "core"), sides)
    in_lanes, in_rows = ((9 * LANES, 3 * LANES), BF16), ((9, 3 * LANES, LANES), BF16)
    weights = call(
        functools.partial(weights_kernel, ch),
        [in_lanes, in_rows, ((1, LANES), F32), ((27, ch, ch), BF16), ((27, ch, ch), BF16)],
        (conv_weight, down_weight, conv_bias.reshape(1, ch)),
        [((1, ch), F32)],
        name="weights",
        vmem=4,
        far=(0, 1, 2),
        sems=3,
    )
    from_core, from_side, *weights = lax.optimization_barrier((from_core, from_side, *weights))
    conv_lanes, down_rows, bias, raw_conv, raw_down = weights
    to_near, to_far = call(
        functools.partial(second_kernel, dims),
        [((row_rows, LANES), BF16)] * 2,
        (x, u, from_core, from_side),
        [((tx, ty + 4, tz, LANES), F32), ((hx, hy + 2, tz, LANES), F32)],
        name="second",
        vmem=4,
    )
    near = [(i, i ^ 1) for i in range(n_gx)]
    far = [(i, i + 1) for i in range(1, n_gx - 1, 2)]
    far += [(j, i) for i, j in far]
    from_far = lax.ppermute(to_far, "gx", far)
    from_near = lax.ppermute(to_near, "gx", near)

    block_rows = ch * ch // LANES
    half_rows = -(-(27 * block_rows + 8) // 64) * 64
    keep, send, gp, gs, s = call(
        functools.partial(main_kernel, dims),
        [((half_rows, LANES), F32), ((half_rows, LANES), BF16)]
        + [((ex * ey * tz, LANES), BF16), ((fine, LANES), F32), ((ex * ey * tz, LANES), BF16)],
        (
            x, u, from_core, from_side, from_near, from_far, conv_lanes, down_rows, bias,
        ),
        [
            ((tx + 4, ty + 4, tz, LANES), F32),
            ((hx + 2, hy + 2, tz, LANES), F32),
            ((hx + 1, 2, hy + 1, 2, tz, LANES), F32),
            ((ex, ey, tz, LANES), F32),
            ((hx + 1, 2, hy + 1, 2, tz, LANES), F32),
            ((ex, ey, tz, LANES), F32),
            ((2, half_rows, LANES), F32),
        ],
        name="main",
        vmem=16,
    )

    rest = call(
        functools.partial(other_weights_kernel, ch),
        [in_rows, in_lanes],
        (raw_conv, raw_down),
        name="weights2",
        vmem=4,
    )
    conv_rows, down_lanes = rest
    down, grad_voxels = call(
        functools.partial(second_outputs, dims),
        [((hx * hy * hz, ch), BF16), ((fine, ch), BF16)],
        (x, u, gp, gs, s, conv_rows, down_lanes),
        [
            ((ex, ey, tz, LANES), F32),
            ((hx + 1, 2, hy + 1, 2, tz, LANES), F32),
            ((coarse, LANES), F32),
        ],
        cost=pl.CostEstimate(flops=5_000_000_000, bytes_accessed=4_000_000, transcendentals=0),
        name="outputs",
        vmem=12,
    )

    def plus(a, b):
        return (a.astype(F32) + b.astype(F32)).astype(BF16)

    got = lax.ppermute(send, "core", swap)
    quarter = half_rows // 4
    mine, *pieces = call(
        split_kernel,
        [((quarter, LANES), F32)] + [((quarter, LANES), BF16)] * 3,
        (keep, got),
        name="split",
        vmem=2,
    )

    def across(value, k):
        route = []
        for i in range(n_gx):
            for j in range(n_gyc):
                route.append((i * n_gyc + j, (i ^ (k >> 1)) * n_gyc + (j ^ (k & 1))))
        return lax.ppermute(value, ("gx", "gyc"), route)

    arrived = [across(piece, k) for k, piece in zip((1, 2, 3), pieces)]
    *arrived, down, grad_voxels = lax.optimization_barrier((*arrived, down, grad_voxels))
    (total,) = call(
        sum_kernel,
        [((quarter, LANES), BF16)],
        (mine, *arrived),
        name="sum",
        vmem=2,
    )
    for axis, peers in (("gx", n_gx), ("gyc", n_gyc)):
        step = 2
        while step < peers:
            total = plus(total, lax.ppermute(total, axis, [(i, i ^ step) for i in range(peers)]))
            step *= 2
    own = [total] + [across(total, k) for k in (1, 2, 3)]
    other = [lax.ppermute(piece, "core", swap) for piece in own]
    factor = 1.0 / math.sqrt(tx * n_gx * ty * n_gy * tz)
    grad_conv, grad_down, grad_bias = call(
        functools.partial(last_kernel, ch, factor),
        [((27, ch, ch), F32), ((27, ch, ch), F32), ((1, ch), F32)],
        (*own, *other),
        [
            ((2, half_rows, LANES), F32),
            ((27, ch, ch), F32),
            ((27, ch, ch), F32),
            ((1, ch), F32),
        ],
        name="last",
        vmem=10,
        far_outs=True,
        sems=7,
    )
    return (
        down.reshape(hx, hy, hz, ch),
        grad_voxels.reshape(tx, ty, tz, ch),
        grad_conv,
        grad_bias.reshape(ch),
        grad_down,
    )


def solution(mesh):
    n_gx, n_gy = mesh.shape["gx"], mesh.shape["gy"]
    split = Mesh(mesh.devices.reshape(n_gx, n_gy // 2, 2), ("gx", "gyc", "core"))
    gy = ("gyc", "core")
    placed = (
        P("gx", gy, None, None),
        P("gx", gy, None),
        P(),
        P(),
        P(),
        P("gx", gy, None, None),
    )
    return jax.shard_map(
        on_device,
        mesh=split,
        in_specs=placed,
        out_specs=(P("gx", gy, None, None), P("gx", gy, None, None), P(), P(), P()),
        check_vma=False,
    )
```

```python
import functools
import math

import jax
import jax.numpy as jnp
from jax import lax
from jax.experimental import pallas as pl
from jax.experimental.pallas import tpu as pltpu
from jax.sharding import Mesh
from jax.sharding import PartitionSpec as P


LANES = 128
F32 = jnp.float32
BF16 = jnp.bfloat16
NT = (((1,), (1,)), ((), ()))
TN = (((0,), (0,)), ((), ()))
MIB = 1024 * 1024


def call(body, outs, args, scratch=(), cost=None, vmem=8, far=(), far_outs=False, sems=0):
    near_spec = pl.BlockSpec(memory_space=pltpu.VMEM)
    far_spec = pl.BlockSpec(memory_space=pltpu.HBM)
    args = [
        pltpu.with_memory_space_constraint(a, pltpu.HBM) if i in far else a
        for i, a in enumerate(args)
    ]
    return pl.pallas_call(
        body,
        out_shape=tuple(jax.ShapeDtypeStruct(s, d) for s, d in outs),
        in_specs=[far_spec if i in far else near_spec for i in range(len(args))],
        out_specs=tuple(far_spec if far_outs else near_spec for _ in outs),
        scratch_shapes=[pltpu.VMEM(s, d) for s, d in scratch]
        + ([pltpu.SemaphoreType.DMA((sems,))] if sems else []),
        compiler_params=pltpu.CompilerParams(vmem_limit_bytes=vmem * MIB),
        cost_estimate=cost,
    )(*args)


def fetch(pairs, sems):
    copies = [pltpu.make_async_copy(a, b, sems.at[i]) for i, (a, b) in enumerate(pairs)]
    for copy in copies:
        copy.start()
    for copy in copies:
        copy.wait()


def lane_of(shape):
    return lax.broadcasted_iota(jnp.int32, shape, len(shape) - 1)


def z_of(shape):
    return lax.broadcasted_iota(jnp.int32, shape, len(shape) - 2)


def below(v):
    return jnp.where(z_of(v.shape) == 0, 0.0, pltpu.roll(v, 1, axis=1))


def above(v):
    top = v.shape[1] - 1
    return jnp.where(z_of(v.shape) == top, 0.0, pltpu.roll(v, top, axis=1))


def first_kernel(
    dims, vox_far, occ_far, cot_far, x_ref, u_ref, core_ref, side_ref,
    xs, us, vox_ref, occ_ref, cot_ref, sems,
):
    tx, ty, tz, ch = dims
    fetch(((vox_far, vox_ref), (occ_far, occ_ref), (cot_far, cot_ref)), sems)
    hx, hy = tx // 2, ty // 2
    occ = jnp.broadcast_to(occ_ref[...].astype(F32)[:, :, None], (tx * ty, tz, LANES))
    xs[...] = jnp.zeros(xs.shape, F32)
    xs[:, :ch] = vox_ref[...].astype(F32)
    x = xs[...].reshape(tx * ty, tz, LANES)
    x = jnp.where(lane_of(x.shape) == ch, 1.0, x) * occ
    xs[...] = x.reshape(xs.shape)
    x_ref[...] = xs[...].astype(BF16)
    pairs = occ.reshape(hx, 2, hy, 2, tz, LANES)
    pairs = jnp.maximum(pairs[:, 0], pairs[:, 1])
    pairs = jnp.maximum(pairs[:, :, 0], pairs[:, :, 1]).reshape(hx * hy, tz, LANES)
    coarse = jnp.maximum(pairs, pltpu.roll(pairs, tz - 1, axis=1))
    us[...] = jnp.zeros(us.shape, F32)
    cot = jnp.concatenate(
        [cot_ref[...].astype(F32), jnp.zeros((hx * hy * tz // 2, LANES - ch), F32)], axis=1
    )
    us[pl.ds(0, hx * hy * tz // 2, stride=2), :] = cot
    u = us[...].reshape(hx * hy, tz, LANES)
    even = lax.rem(z_of(u.shape), 2) == 0
    u = jnp.where((lane_of(u.shape) == ch) & even, 1.0, u) * coarse
    us[...] = u.reshape(us.shape)
    u_ref[...] = us[...].astype(BF16)
    core = lax.axis_index("core")
    x4, u4 = xs.reshape(tx, ty, tz, LANES), us.reshape(hx, hy, tz, LANES)
    rows = tx * 2 * tz
    for ref, low in ((core_ref, core), (side_ref, 1 - core)):
        start = (1 - low) * (ty - 2)
        ref[:rows] = x4[:, pl.ds(start, 2)].reshape(rows, LANES).astype(BF16)
        ref[rows:] = (
            u4[:, pl.ds((1 - low) * (hy - 1), 1)].reshape(hx * tz, LANES).astype(BF16)
        )


def second_kernel(dims, x_ref, u_ref, core_ref, side_ref, near_ref, far_ref, xe, ue):
    tx, ty, tz, _ = dims
    widen(dims, x_ref, u_ref, core_ref, side_ref, xe, ue, 0, 0)
    odd = lax.rem(lax.axis_index("gx"), 2)
    rows = 2 * (ty + 4) * tz
    hx, hy = tx // 2, ty // 2
    for ref, low in ((near_ref, odd), (far_ref, 1 - odd)):
        ref[:rows] = xe[pl.ds((1 - low) * (tx - 2), 2)].reshape(rows, LANES).astype(BF16)
        ref[rows:] = (
            ue[pl.ds((1 - low) * (hx - 1), 1)].reshape((hy + 2) * tz, LANES).astype(BF16)
        )


def widen(dims, x_ref, u_ref, core_ref, side_ref, xe, ue, x0, u0):
    tx, ty, tz, _ = dims
    hx, hy = tx // 2, ty // 2
    rows = tx * 2 * tz
    core = lax.axis_index("core")
    xe[x0 : x0 + tx, 2 : 2 + ty] = x_ref[...].astype(F32).reshape(tx, ty, tz, LANES)
    ue[u0 : u0 + hx, 1 : 1 + hy] = u_ref[...].astype(F32).reshape(hx, hy, tz, LANES)
    for ref, low in ((core_ref, core), (side_ref, 1 - core)):
        xe[x0 : x0 + tx, pl.ds((1 - low) * (ty + 2), 2)] = (
            ref[:rows].astype(F32).reshape(tx, 2, tz, LANES)
        )
        ue[u0 : u0 + hx, pl.ds((1 - low) * (hy + 1), 1)] = (
            ref[rows:].astype(F32).reshape(hx, 1, tz, LANES)
        )


def taps_in_rows(ch, w_ref, out):
    out[...] = jnp.zeros(out.shape, BF16)
    for t in range(w_ref.shape[0]):
        out[t // 3, (t % 3) * LANES : (t % 3) * LANES + ch, :ch] = w_ref[t]


def taps_in_lanes(ch, w_ref, out):
    out[...] = jnp.zeros(out.shape, BF16)
    for t in range(w_ref.shape[0]):
        at, lane = t // 3 * LANES, t % 3 * LANES
        out[at : at + ch, lane : lane + ch] = w_ref[t]


def weights_kernel(ch, cw_far, dw_far, bias_far, cl_ref, dr_ref, b_ref, cw, dw, bias, sems):
    fetch(((cw_far, cw), (dw_far, dw), (bias_far, bias)), sems)
    taps_in_lanes(ch, cw, cl_ref)
    taps_in_rows(ch, dw, dr_ref)
    b_ref[...] = jnp.zeros(b_ref.shape, F32)
    b_ref[:, :ch] = bias[...]


def other_weights_kernel(ch, cw, dw, cr_ref, dl_ref):
    taps_in_rows(ch, cw, cr_ref)
    taps_in_lanes(ch, dw, dl_ref)


def three(v):
    return v[:, :, :LANES], v[:, :, LANES : 2 * LANES], v[:, :, 2 * LANES :]


def pack_block(block, ch):
    free = LANES - ch
    keep = ch * ch // LANES
    tail = block[keep:ch]
    parts = [
        pltpu.roll(tail, (LANES - free - p * free) % LANES, axis=1) for p in range(ch // free)
    ]
    parts = jnp.concatenate(parts, axis=0)
    main = block[:keep]
    return jnp.where(lane_of(main.shape) < ch, main, parts)


def unpack_block(packed, ch):
    free = LANES - ch
    keep = ch * ch // LANES
    tall = ch - keep
    lane = lane_of((tall, LANES))
    tail = None
    for p in range(ch // free):
        part = packed[p * tall : (p + 1) * tall]
        part = pltpu.roll(part, (free + p * free) % LANES, axis=1)
        tail = part if tail is None else jnp.where(lane < p * free, tail, part)
    return jnp.concatenate([packed, tail], axis=0)


def fine_gradient(rows, wd, picks):
    wins = [win.reshape(rows, LANES).astype(BF16) for _, win, _ in picks]
    taps = [wd[a * 3 + b] for a, _, b in picks]
    return lax.dot_general(
        jnp.concatenate(wins, axis=1), jnp.concatenate(taps, axis=1), NT,
        preferred_element_type=F32,
    )


def z_sum(out, lower, upper):
    low, same, high = three(out)
    return lower(low) + same + upper(high)


def unit(v, bias, x, g, ch):
    v = v + bias[...].reshape(1, 1, LANES)
    live = jnp.broadcast_to(x[:, :, ch : ch + 1], x.shape)
    s = 1.0 / (1.0 + jnp.exp(-v))
    summed = (x + live * (v * s)).astype(BF16).astype(F32)
    grad = (g * live * s * (1.0 + v * (1.0 - s))).astype(BF16).astype(F32)
    return summed, grad


def with_ones(win, a, b, ch):
    if a == 1 and b == 1:
        win = jnp.where(lane_of(win.shape) == ch + 1, 1.0, win)
    return win


def z_taps(other):
    cells = other.shape[0] * other.shape[1]
    other = jnp.concatenate([above(other), other, below(other)], axis=2)
    return other.reshape(cells, 3 * LANES).astype(BF16)


TERMS = {0: ((2, 0), (0, 1)), 1: ((1, 1),)}


def inner_kernel(
    dims, x_ref, u_ref, core_ref, side_ref, wf, wd, bias, gp_ref, s_ref, gs_ref, acc_ref,
    xe, ue, pre, gsr, gp,
):
    tx, ty, tz, ch = dims
    hx, hy = tx // 2, ty // 2
    ey, inner = ty + 2, tx - 2
    widen(dims, x_ref, u_ref, core_ref, side_ref, xe, ue, 0, 0)
    wins = [
        xe[a : a + inner, b : b + ey].reshape(inner * ey * tz, LANES).astype(BF16)
        for a in range(3)
        for b in range(3)
    ]
    out = jnp.dot(jnp.concatenate(wins, axis=1), wf[...], preferred_element_type=F32)
    out = z_sum(out.reshape(inner * ey, tz, 3 * LANES), below, above)
    pre[...] = out.reshape(inner, ey, tz, LANES)
    for px in (0, 1):
        for py in (0, 1):
            picks = [
                (a, ue[sx : sx + hx - 1, sy : sy + hy + 1], b)
                for a, sx in TERMS[px]
                for b, sy in TERMS[py]
            ]
            out = fine_gradient((hx - 1) * (hy + 1) * tz, wd, picks)
            out = z_sum(out.reshape((hx - 1) * (hy + 1), tz, 3 * LANES), above, below)
            gsr[:, px, :, py] = out.reshape(hx - 1, hy + 1, tz, LANES)

    def pointwise(i, _):
        g = gsr[i // 2, lax.rem(i, 2)].reshape(ey, tz, LANES)
        summed, grad = unit(pre[i], bias, xe[i + 1, 1 : 1 + ey], g, ch)
        at = pl.ds(pl.multiple_of(i * ey * tz, 16), ey * tz)
        s_ref[at] = summed.reshape(ey * tz, LANES).astype(BF16)
        gp_ref[at] = grad.reshape(ey * tz, LANES).astype(BF16)
        gp[i] = grad
        return 0

    lax.fori_loop(0, inner, pointwise, 0)
    gs_ref[...] = gsr[...].reshape(inner, ey, tz, LANES)[:, 1 : 1 + ty].reshape(
        inner * ty * tz, LANES
    )
    other = z_taps(gp[:, 1 : 1 + ty].reshape(inner * ty, tz, LANES))
    for a in range(3):
        wins = [
            with_ones(xe[a : a + inner, b + 1 : b + 1 + ty], a, b, ch)
            .reshape(inner * ty * tz, LANES)
            .astype(BF16)
            for b in range(3)
        ]
        acc_ref[a * 3 * LANES : (a + 1) * 3 * LANES] = lax.dot_general(
            jnp.concatenate(wins, axis=1), other, TN, preferred_element_type=F32
        )


def main_kernel(
    dims, x_ref, u_ref, core_ref, side_ref, near_ref, far_ref, wf, wd, bias, gpa_ref, sa_ref, acc_ref,
    keep_ref, send_ref, gpb_ref, sb_ref, gsb_ref,
    xe, ue, ss, pre, gsr, edge, pack,
):
    tx, ty, tz, ch = dims
    hx, hy = tx // 2, ty // 2
    ex, ey = tx + 2, ty + 2
    slab = ey * tz
    block_rows = ch * ch // LANES
    core = lax.axis_index("core")
    odd = lax.rem(lax.axis_index("gx"), 2)
    widen(dims, x_ref, u_ref, core_ref, side_ref, xe, ue, 2, 1)
    rows = 2 * (ty + 4) * tz
    for ref, low in ((near_ref, odd), (far_ref, 1 - odd)):
        xe[pl.ds((1 - low) * (tx + 2), 2)] = ref[:rows].astype(F32).reshape(2, ty + 4, tz, LANES)
        ue[pl.ds((1 - low) * (hx + 1), 1)] = ref[rows:].astype(F32).reshape(1, hy + 2, tz, LANES)
    ss[1:hx] = sa_ref[...].astype(F32).reshape(hx - 1, 2, hy + 1, 2, tz, LANES)

    def edges(v, a, lower, upper):
        return jnp.concatenate([v[lower + a : lower + a + 2], v[upper + a : upper + a + 2]], axis=0)

    wins = [
        edges(xe, a, 0, ex - 2)[:, b : b + ey].reshape(4 * slab, LANES).astype(BF16)
        for a in range(3)
        for b in range(3)
    ]
    out = jnp.dot(jnp.concatenate(wins, axis=1), wf[...], preferred_element_type=F32)
    out = z_sum(out.reshape(4 * ey, tz, 3 * LANES), below, above)
    pre[...] = out.reshape(4, ey, tz, LANES)
    for px in (0, 1):
        for py in (0, 1):
            picks = []
            for a, sx in TERMS[px]:
                for b, sy in TERMS[py]:
                    win = jnp.concatenate(
                        [ue[sx, sy : sy + hy + 1], ue[hx + sx, sy : sy + hy + 1]], axis=0
                    )
                    picks.append((a, win, b))
            out = fine_gradient(2 * (hy + 1) * tz, wd, picks)
            out = z_sum(out.reshape(2 * (hy + 1), tz, 3 * LANES), above, below)
            gsr[:, px, :, py] = out.reshape(2, hy + 1, tz, LANES)
    for j, i in enumerate((0, 1, ex - 2, ex - 1)):
        g = gsr[j // 2, j % 2].reshape(ey, tz, LANES)
        summed, grad = unit(pre[j], bias, xe[i + 1, 1 : 1 + ey], g, ch)
        ss[i // 2, i % 2] = summed.reshape(hy + 1, 2, tz, LANES)
        sb_ref[j * slab : (j + 1) * slab] = summed.reshape(slab, LANES).astype(BF16)
        gpb_ref[j * slab : (j + 1) * slab] = grad.reshape(slab, LANES).astype(BF16)
        if j in (1, 2):
            edge[j - 1] = grad[1 : 1 + ty]
            gsb_ref[(j - 1) * ty * tz : j * ty * tz] = g[1 : 1 + ty].reshape(ty * tz, LANES)

    def gradients(h, wins, other, before):
        for a in range(3):
            win = jnp.concatenate([wins(a, b) for b in range(3)], axis=1)
            out = lax.dot_general(win, other, TN, preferred_element_type=F32)
            if before is not None:
                out = out + before[a * 3 * LANES : (a + 1) * 3 * LANES]
            for b in range(3):
                for e in range(3):
                    at = (a * 9 + b * 3 + e) * block_rows
                    block = out[b * LANES : b * LANES + ch, e * LANES : (e + 1) * LANES]
                    pack[h, at : at + block_rows] = pack_block(block, ch)
            if a == 1:
                at = 27 * block_rows
                pack[h, at : at + 8] = out[LANES + ch : LANES + ch + 8, LANES : 2 * LANES]
        at = 27 * block_rows + 8
        pack[h, at:] = jnp.zeros((pack.shape[1] - at, LANES), F32)

    def fine_window(a, b):
        win = jnp.concatenate(
            [xe[a + 1, b + 1 : b + 1 + ty], xe[tx + a, b + 1 : b + 1 + ty]], axis=0
        )
        return with_ones(win, a, b, ch).reshape(2 * ty * tz, LANES).astype(BF16)

    def coarse_window(a, b):
        win = ss[a // 2 : a // 2 + hx, a % 2, b // 2 : b // 2 + hy, b % 2]
        return win.reshape(hx * hy * tz, LANES).astype(BF16)

    gradients(0, fine_window, z_taps(edge[...].reshape(2 * ty, tz, LANES)), acc_ref)
    own = ue[1 : 1 + hx, 1 : 1 + hy].reshape(hx * hy, tz, LANES)
    gradients(1, coarse_window, z_taps(own), None)
    keep_ref[...] = pack[core]
    send_ref[...] = pack[1 - core].astype(BF16)


def second_outputs(
    dims, x_ref, u_ref, gpa_ref, gpb_ref, gsa_ref, gsb_ref, sa_ref, sb_ref, wf, wd, down_ref, gv_ref,
    ge, ss, accd,
):
    tx, ty, tz, ch = dims
    hx, hy = tx // 2, ty // 2
    ex, ey = tx + 2, ty + 2
    slab = ey * tz
    ge[2:tx] = gpa_ref[...].astype(F32).reshape(tx - 2, ey, tz, LANES)
    ss[1:hx] = sa_ref[...].astype(F32).reshape(hx - 1, 2, hy + 1, 2, tz, LANES)
    for j, i in enumerate((0, 1, ex - 2, ex - 1)):
        ge[i] = gpb_ref[j * slab : (j + 1) * slab].astype(F32).reshape(ey, tz, LANES)
        ss[i // 2, i % 2] = (
            sb_ref[j * slab : (j + 1) * slab].astype(F32).reshape(hy + 1, 2, tz, LANES)
        )
    wins = [
        ss[a // 2 : a // 2 + hx, a % 2, b // 2 : b // 2 + hy, b % 2]
        .reshape(hx * hy * tz, LANES)
        .astype(BF16)
        for a in range(3)
        for b in range(3)
    ]
    out = jnp.dot(jnp.concatenate(wins, axis=1), wd[...], preferred_element_type=F32)
    out = z_sum(out.reshape(hx * hy, tz, 3 * LANES), below, above).reshape(hx * hy * tz, LANES)
    u = u_ref[...].astype(F32)
    accd[...] = out * jnp.broadcast_to(u[:, ch : ch + 1], u.shape)
    down_ref[...] = accd[pl.ds(0, hx * hy * tz // 2, stride=2), :][:, :ch].astype(BF16)

    wins = [
        ge[2 - a : 2 - a + tx, 2 - b : 2 - b + ty].reshape(tx * ty * tz, LANES).astype(BF16)
        for a in range(3)
        for b in range(3)
    ]
    taps = jnp.concatenate([wf[ab] for ab in range(9)], axis=1)
    out = lax.dot_general(jnp.concatenate(wins, axis=1), taps, NT, preferred_element_type=F32)
    out = z_sum(out.reshape(tx * ty, tz, 3 * LANES), above, below).reshape(tx * ty * tz, LANES)
    x = x_ref[...].astype(F32)
    live = jnp.broadcast_to(x[:, ch : ch + 1], x.shape)
    column = ty * tz
    grad = jnp.concatenate([gsb_ref[:column], gsa_ref[...], gsb_ref[column:]], axis=0)
    gv_ref[...] = ((grad + out) * live)[:, :ch].astype(BF16)


def split_kernel(keep_ref, got_ref, own_ref, *to_refs):
    me = lax.rem(lax.axis_index("gx"), 2) * 2 + lax.rem(lax.axis_index("gyc"), 2)
    rows = own_ref.shape[0]
    for k, ref in enumerate((own_ref, *to_refs)):
        at = pl.ds(pl.multiple_of((me ^ k) * rows, 16), rows)
        ref[...] = (keep_ref[at] + got_ref[at].astype(F32)).astype(ref.dtype)


def sum_kernel(own_ref, a_ref, b_ref, c_ref, out_ref):
    out_ref[...] = (
        own_ref[...] + a_ref[...].astype(F32) + b_ref[...].astype(F32) + c_ref[...].astype(F32)
    ).astype(BF16)


def last_kernel(ch, factor, *refs):
    own, other = refs[:4], refs[4:8]
    conv_ref, down_ref, bias_ref, full, conv_out, down_out, bias_out, sems = refs[8:]
    core = lax.axis_index("core")
    me = lax.rem(lax.axis_index("gx"), 2) * 2 + lax.rem(lax.axis_index("gyc"), 2)
    rows = own[0].shape[0]
    block_rows = ch * ch // LANES
    for k in range(4):
        at = pl.ds(pl.multiple_of((me ^ k) * rows, 16), rows)
        full[core, at] = own[k][...].astype(F32) * factor
        full[1 - core, at] = other[k][...].astype(F32) * factor
    bias_out[...] = full[0, 27 * block_rows + 1 : 27 * block_rows + 2, :ch]
    copies = [pltpu.make_async_copy(bias_out, bias_ref, sems.at[0])]
    copies[0].start()
    for h, ref, out in ((0, conv_ref, conv_out), (1, down_ref, down_out)):
        for a in range(3):
            for t in range(a * 9, a * 9 + 9):
                block = unpack_block(full[h, t * block_rows : (t + 1) * block_rows], ch)
                out[t] = block[:, :ch]
            part = pl.ds(a * 9, 9)
            copy = pltpu.make_async_copy(out.at[part], ref.at[part], sems.at[1 + h * 3 + a])
            copy.start()
            copies.append(copy)
    for copy in copies:
        copy.wait()


def on_device(voxels, occupancy, conv_weight, conv_bias, down_weight, down_cotangent):
    tx, ty, tz, ch = voxels.shape
    hx, hy, hz = tx // 2, ty // 2, tz // 2
    ex, ey = tx + 2, ty + 2
    dims = (tx, ty, tz, ch)
    n_gx, n_gyc = lax.axis_size("gx"), lax.axis_size("gyc")
    fine, coarse = tx * ty * tz, hx * hy * tz

    side_rows = tx * 2 * tz + hx * tz
    row_rows = 2 * (ty + 4) * tz + (hy + 2) * tz
    x, u, to_core, to_side = call(
        functools.partial(first_kernel, dims),
        [((fine, LANES), BF16), ((coarse, LANES), BF16)] + [((side_rows, LANES), BF16)] * 2,
        (
            voxels.reshape(fine, ch),
            occupancy.reshape(tx * ty, tz),
            down_cotangent.reshape(hx * hy * hz, ch),
        ),
        [
            ((fine, LANES), F32),
            ((coarse, LANES), F32),
            ((fine, ch), BF16),
            ((tx * ty, tz), jnp.int32),
            ((hx * hy * hz, ch), BF16),
        ],
        vmem=4,
        far=(0, 1, 2),
        sems=3,
    )
    swap = [(0, 1), (1, 0)]
    n_gy = n_gyc * 2
    sides = [(i, i + 1) for i in range(1, n_gy - 1, 2)]
    sides += [(j, i) for i, j in sides]
    from_core = lax.ppermute(to_core, "core", swap)
    from_side = lax.ppermute(to_side, ("gyc", "core"), sides)
    in_lanes, in_rows = ((9 * LANES, 3 * LANES), BF16), ((9, 3 * LANES, LANES), BF16)
    weights = call(
        functools.partial(weights_kernel, ch),
        [in_lanes, in_rows, ((1, LANES), F32), ((27, ch, ch), BF16), ((27, ch, ch), BF16)],
        (conv_weight, down_weight, conv_bias.reshape(1, ch)),
        [((1, ch), F32)],
        vmem=4,
        far=(0, 1, 2),
        sems=3,
    )
    from_core, from_side, *weights = lax.optimization_barrier((from_core, from_side, *weights))
    conv_lanes, down_rows, bias, raw_conv, raw_down = weights
    to_near, to_far = call(
        functools.partial(second_kernel, dims),
        [((row_rows, LANES), BF16)] * 2,
        (x, u, from_core, from_side),
        [((tx, ty + 4, tz, LANES), F32), ((hx, hy + 2, tz, LANES), F32)],
        vmem=4,
    )
    near = [(i, i ^ 1) for i in range(n_gx)]
    far = [(i, i + 1) for i in range(1, n_gx - 1, 2)]
    far += [(j, i) for i, j in far]
    from_near = lax.ppermute(to_near, "gx", near)
    from_far = lax.ppermute(to_far, "gx", far)
    inner = tx - 2
    *results, = call(
        functools.partial(inner_kernel, dims),
        [((inner * ey * tz, LANES), BF16)] * 2
        + [((inner * ty * tz, LANES), F32), ((9 * LANES, 3 * LANES), F32)],
        (x, u, from_core, from_side, conv_lanes, down_rows, bias),
        [
            ((tx, ty + 4, tz, LANES), F32),
            ((hx, hy + 2, tz, LANES), F32),
            ((inner, ey, tz, LANES), F32),
            ((hx - 1, 2, hy + 1, 2, tz, LANES), F32),
            ((inner, ey, tz, LANES), F32),
        ],
        cost=pl.CostEstimate(flops=5_000_000_000, bytes_accessed=4_000_000, transcendentals=0),
        vmem=12,
    )
    from_far, from_near, *results = lax.optimization_barrier((from_far, from_near, *results))
    gp_inner, s_inner, gs_inner, acc = results

    block_rows = ch * ch // LANES
    half_rows = -(-(27 * block_rows + 8) // 64) * 64
    keep, send, gp_edge, s_edge, gs_edge = call(
        functools.partial(main_kernel, dims),
        [((half_rows, LANES), F32), ((half_rows, LANES), BF16)]
        + [((4 * ey * tz, LANES), BF16)] * 2
        + [((2 * ty * tz, LANES), F32)],
        (
            x, u, from_core, from_side, from_near, from_far, conv_lanes, down_rows, bias,
            gp_inner, s_inner, acc,
        ),
        [
            ((tx + 4, ty + 4, tz, LANES), F32),
            ((hx + 2, hy + 2, tz, LANES), F32),
            ((hx + 1, 2, hy + 1, 2, tz, LANES), F32),
            ((4, ey, tz, LANES), F32),
            ((2, 2, hy + 1, 2, tz, LANES), F32),
            ((2, ty, tz, LANES), F32),
            ((2, half_rows, LANES), F32),
        ],
        vmem=16,
    )

    rest = call(
        functools.partial(other_weights_kernel, ch),
        [in_rows, in_lanes],
        (raw_conv, raw_down),
        vmem=4,
    )
    conv_rows, down_lanes = rest
    down, grad_voxels = call(
        functools.partial(second_outputs, dims),
        [((hx * hy * hz, ch), BF16), ((fine, ch), BF16)],
        (x, u, gp_inner, gp_edge, gs_inner, gs_edge, s_inner, s_edge, conv_rows, down_lanes),
        [
            ((ex, ey, tz, LANES), F32),
            ((hx + 1, 2, hy + 1, 2, tz, LANES), F32),
            ((coarse, LANES), F32),
        ],
        cost=pl.CostEstimate(flops=5_000_000_000, bytes_accessed=4_000_000, transcendentals=0),
        vmem=12,
    )

    def plus(a, b):
        return (a.astype(F32) + b.astype(F32)).astype(BF16)

    got = lax.ppermute(send, "core", swap)
    quarter = half_rows // 4
    mine, *pieces = call(
        split_kernel,
        [((quarter, LANES), F32)] + [((quarter, LANES), BF16)] * 3,
        (keep, got),
        vmem=2,
    )

    def across(value, k):
        route = []
        for i in range(n_gx):
            for j in range(n_gyc):
                route.append((i * n_gyc + j, (i ^ (k >> 1)) * n_gyc + (j ^ (k & 1))))
        return lax.ppermute(value, ("gx", "gyc"), route)

    arrived = [across(piece, k) for k, piece in zip((1, 2, 3), pieces)]
    *arrived, down, grad_voxels = lax.optimization_barrier((*arrived, down, grad_voxels))
    (total,) = call(sum_kernel, [((quarter, LANES), BF16)], (mine, *arrived), vmem=2)
    for axis, peers in (("gx", n_gx), ("gyc", n_gyc)):
        step = 2
        while step < peers:
            total = plus(total, lax.ppermute(total, axis, [(i, i ^ step) for i in range(peers)]))
            step *= 2
    own = [total] + [across(total, k) for k in (1, 2, 3)]
    other = []
    for piece in own:
        other.append(lax.ppermute(piece, "core", swap))
    factor = 1.0 / math.sqrt(tx * n_gx * ty * n_gy * tz)
    grad_conv, grad_down, grad_bias = call(
        functools.partial(last_kernel, ch, factor),
        [((27, ch, ch), F32), ((27, ch, ch), F32), ((1, ch), F32)],
        (*own, *other),
        [
            ((2, half_rows, LANES), F32),
            ((27, ch, ch), F32),
            ((27, ch, ch), F32),
            ((1, ch), F32),
        ],
        vmem=10,
        far_outs=True,
        sems=7,
    )
    return (
        down.reshape(hx, hy, hz, ch),
        grad_voxels.reshape(tx, ty, tz, ch),
        grad_conv,
        grad_bias.reshape(ch),
        grad_down,
    )


def solution(mesh):
    n_gx, n_gy = mesh.shape["gx"], mesh.shape["gy"]
    split = Mesh(mesh.devices.reshape(n_gx, n_gy // 2, 2), ("gx", "gyc", "core"))
    gy = ("gyc", "core")
    placed = (
        P("gx", gy, None, None),
        P("gx", gy, None),
        P(),
        P(),
        P(),
        P("gx", gy, None, None),
    )

    return jax.shard_map(
        on_device,
        mesh=split,
        in_specs=placed,
        out_specs=(P("gx", gy, None, None), P("gx", gy, None, None), P(), P(), P()),
        check_vma=False,
    )
```

```python
import functools
import math

import jax
import jax.numpy as jnp
from jax import lax
from jax.experimental import pallas as pl
from jax.experimental.pallas import tpu as pltpu
from jax.sharding import Mesh
from jax.sharding import PartitionSpec as P


LANES = 128
F32 = jnp.float32
BF16 = jnp.bfloat16
NT = (((1,), (1,)), ((), ()))
TN = (((0,), (0,)), ((), ()))
MIB = 1024 * 1024


def call(body, outs, args, scratch=(), cost=None, vmem=8, far=(), far_outs=False, sems=0):
    near_spec = pl.BlockSpec(memory_space=pltpu.VMEM)
    far_spec = pl.BlockSpec(memory_space=pltpu.HBM)
    args = [
        pltpu.with_memory_space_constraint(a, pltpu.HBM) if i in far else a
        for i, a in enumerate(args)
    ]
    return pl.pallas_call(
        body,
        out_shape=tuple(jax.ShapeDtypeStruct(s, d) for s, d in outs),
        in_specs=[far_spec if i in far else near_spec for i in range(len(args))],
        out_specs=tuple(far_spec if far_outs else near_spec for _ in outs),
        scratch_shapes=[pltpu.VMEM(s, d) for s, d in scratch]
        + ([pltpu.SemaphoreType.DMA((sems,))] if sems else []),
        compiler_params=pltpu.CompilerParams(vmem_limit_bytes=vmem * MIB),
        cost_estimate=cost,
    )(*args)


def fetch(pairs, sems):
    copies = [pltpu.make_async_copy(a, b, sems.at[i]) for i, (a, b) in enumerate(pairs)]
    for copy in copies:
        copy.start()
    for copy in copies:
        copy.wait()


def lane_of(shape):
    return lax.broadcasted_iota(jnp.int32, shape, len(shape) - 1)


def z_of(shape):
    return lax.broadcasted_iota(jnp.int32, shape, len(shape) - 2)


def below(v):
    return jnp.where(z_of(v.shape) == 0, 0.0, pltpu.roll(v, 1, axis=1))


def above(v):
    top = v.shape[1] - 1
    return jnp.where(z_of(v.shape) == top, 0.0, pltpu.roll(v, top, axis=1))


def first_kernel(
    dims, vox_far, occ_far, cot_far, x_ref, u_ref, core_ref, side_ref,
    xs, us, vox_ref, occ_ref, cot_ref, sems,
):
    tx, ty, tz, ch = dims
    fetch(((vox_far, vox_ref), (occ_far, occ_ref), (cot_far, cot_ref)), sems)
    hx, hy = tx // 2, ty // 2
    occ = jnp.broadcast_to(occ_ref[...].astype(F32)[:, :, None], (tx * ty, tz, LANES))
    xs[...] = jnp.zeros(xs.shape, F32)
    xs[:, :ch] = vox_ref[...].astype(F32)
    x = xs[...].reshape(tx * ty, tz, LANES)
    x = jnp.where(lane_of(x.shape) == ch, 1.0, x) * occ
    xs[...] = x.reshape(xs.shape)
    x_ref[...] = xs[...].astype(BF16)
    pairs = occ.reshape(hx, 2, hy, 2, tz, LANES)
    pairs = jnp.maximum(pairs[:, 0], pairs[:, 1])
    pairs = jnp.maximum(pairs[:, :, 0], pairs[:, :, 1]).reshape(hx * hy, tz, LANES)
    coarse = jnp.maximum(pairs, pltpu.roll(pairs, tz - 1, axis=1))
    us[...] = jnp.zeros(us.shape, F32)
    cot = jnp.concatenate(
        [cot_ref[...].astype(F32), jnp.zeros((hx * hy * tz // 2, LANES - ch), F32)], axis=1
    )
    us[pl.ds(0, hx * hy * tz // 2, stride=2), :] = cot
    u = us[...].reshape(hx * hy, tz, LANES)
    even = lax.rem(z_of(u.shape), 2) == 0
    u = jnp.where((lane_of(u.shape) == ch) & even, 1.0, u) * coarse
    us[...] = u.reshape(us.shape)
    u_ref[...] = us[...].astype(BF16)
    core = lax.axis_index("core")
    x4, u4 = xs.reshape(tx, ty, tz, LANES), us.reshape(hx, hy, tz, LANES)
    rows = tx * 2 * tz
    for ref, low in ((core_ref, core), (side_ref, 1 - core)):
        start = (1 - low) * (ty - 2)
        ref[:rows] = x4[:, pl.ds(start, 2)].reshape(rows, LANES).astype(BF16)
        ref[rows:] = (
            u4[:, pl.ds((1 - low) * (hy - 1), 1)].reshape(hx * tz, LANES).astype(BF16)
        )


def second_kernel(dims, x_ref, u_ref, core_ref, side_ref, near_ref, far_ref, xe, ue):
    tx, ty, tz, _ = dims
    widen(dims, x_ref, u_ref, core_ref, side_ref, xe, ue, 0, 0)
    odd = lax.rem(lax.axis_index("gx"), 2)
    rows = 2 * (ty + 4) * tz
    hx, hy = tx // 2, ty // 2
    for ref, low in ((near_ref, odd), (far_ref, 1 - odd)):
        ref[:rows] = xe[pl.ds((1 - low) * (tx - 2), 2)].reshape(rows, LANES).astype(BF16)
        ref[rows:] = (
            ue[pl.ds((1 - low) * (hx - 1), 1)].reshape((hy + 2) * tz, LANES).astype(BF16)
        )


def widen(dims, x_ref, u_ref, core_ref, side_ref, xe, ue, x0, u0):
    tx, ty, tz, _ = dims
    hx, hy = tx // 2, ty // 2
    rows = tx * 2 * tz
    core = lax.axis_index("core")
    xe[x0 : x0 + tx, 2 : 2 + ty] = x_ref[...].astype(F32).reshape(tx, ty, tz, LANES)
    ue[u0 : u0 + hx, 1 : 1 + hy] = u_ref[...].astype(F32).reshape(hx, hy, tz, LANES)
    inside = in_grid(1 - core, "gyc")
    for ref, low, real in ((core_ref, core, True), (side_ref, 1 - core, inside)):
        part = jnp.where(real, ref[...].astype(F32), 0.0)
        xe[x0 : x0 + tx, pl.ds((1 - low) * (ty + 2), 2)] = part[:rows].reshape(tx, 2, tz, LANES)
        ue[u0 : u0 + hx, pl.ds((1 - low) * (hy + 1), 1)] = part[rows:].reshape(hx, 1, tz, LANES)


def in_grid(low, axis):
    me = lax.axis_index(axis)
    return jnp.where(low == 1, me > 0, me < lax.axis_size(axis) - 1)


def taps_in_rows(ch, w_ref, out):
    out[...] = jnp.zeros(out.shape, BF16)
    for t in range(w_ref.shape[0]):
        out[t // 3, (t % 3) * LANES : (t % 3) * LANES + ch, :ch] = w_ref[t]


def taps_in_lanes(ch, w_ref, out):
    out[...] = jnp.zeros(out.shape, BF16)
    for t in range(w_ref.shape[0]):
        at, lane = t // 3 * LANES, t % 3 * LANES
        out[at : at + ch, lane : lane + ch] = w_ref[t]


def weights_kernel(ch, cw_far, dw_far, bias_far, cl_ref, dr_ref, b_ref, cw, dw, bias, sems):
    fetch(((cw_far, cw), (dw_far, dw), (bias_far, bias)), sems)
    taps_in_lanes(ch, cw, cl_ref)
    taps_in_rows(ch, dw, dr_ref)
    b_ref[...] = jnp.zeros(b_ref.shape, F32)
    b_ref[:, :ch] = bias[...]


def other_weights_kernel(ch, cw, dw, cr_ref, dl_ref):
    taps_in_rows(ch, cw, cr_ref)
    taps_in_lanes(ch, dw, dl_ref)


def three(v):
    return v[:, :, :LANES], v[:, :, LANES : 2 * LANES], v[:, :, 2 * LANES :]


def pack_block(block, ch):
    free = LANES - ch
    keep = ch * ch // LANES
    tail = block[keep:ch]
    parts = [
        pltpu.roll(tail, (LANES - free - p * free) % LANES, axis=1) for p in range(ch // free)
    ]
    parts = jnp.concatenate(parts, axis=0)
    main = block[:keep]
    return jnp.where(lane_of(main.shape) < ch, main, parts)


def unpack_block(packed, ch):
    free = LANES - ch
    keep = ch * ch // LANES
    tall = ch - keep
    lane = lane_of((tall, LANES))
    tail = None
    for p in range(ch // free):
        part = packed[p * tall : (p + 1) * tall]
        part = pltpu.roll(part, (free + p * free) % LANES, axis=1)
        tail = part if tail is None else jnp.where(lane < p * free, tail, part)
    return jnp.concatenate([packed, tail], axis=0)


def fine_gradient(rows, wd, picks):
    wins = [win.reshape(rows, LANES).astype(BF16) for _, win, _ in picks]
    taps = [wd[a * 3 + b] for a, _, b in picks]
    return lax.dot_general(
        jnp.concatenate(wins, axis=1), jnp.concatenate(taps, axis=1), NT,
        preferred_element_type=F32,
    )


def z_sum(out, lower, upper):
    low, same, high = three(out)
    return lower(low) + same + upper(high)


def unit(v, bias, x, g, ch):
    v = v + bias[...].reshape(1, 1, LANES)
    live = jnp.broadcast_to(x[:, :, ch : ch + 1], x.shape)
    s = 1.0 / (1.0 + jnp.exp(-v))
    summed = (x + live * (v * s)).astype(BF16).astype(F32)
    grad = (g * live * s * (1.0 + v * (1.0 - s))).astype(BF16).astype(F32)
    return summed, grad


def with_ones(win, a, b, ch):
    if a == 1 and b == 1:
        win = jnp.where(lane_of(win.shape) == ch + 1, 1.0, win)
    return win


def z_taps(other):
    cells = other.shape[0] * other.shape[1]
    other = jnp.concatenate([above(other), other, below(other)], axis=2)
    return other.reshape(cells, 3 * LANES).astype(BF16)


TERMS = {0: ((2, 0), (0, 1)), 1: ((1, 1),)}


def inner_kernel(
    dims, x_ref, u_ref, core_ref, side_ref, wf, wd, bias, gp_ref, s_ref, gs_ref, acc_ref,
    xe, ue, pre, gsr, gp,
):
    tx, ty, tz, ch = dims
    hx, hy = tx // 2, ty // 2
    ey, inner = ty + 2, tx - 2
    widen(dims, x_ref, u_ref, core_ref, side_ref, xe, ue, 0, 0)
    wins = [
        xe[a : a + inner, b : b + ey].reshape(inner * ey * tz, LANES).astype(BF16)
        for a in range(3)
        for b in range(3)
    ]
    out = jnp.dot(jnp.concatenate(wins, axis=1), wf[...], preferred_element_type=F32)
    out = z_sum(out.reshape(inner * ey, tz, 3 * LANES), below, above)
    pre[...] = out.reshape(inner, ey, tz, LANES)
    for px in (0, 1):
        for py in (0, 1):
            picks = [
                (a, ue[sx : sx + hx - 1, sy : sy + hy + 1], b)
                for a, sx in TERMS[px]
                for b, sy in TERMS[py]
            ]
            out = fine_gradient((hx - 1) * (hy + 1) * tz, wd, picks)
            out = z_sum(out.reshape((hx - 1) * (hy + 1), tz, 3 * LANES), above, below)
            gsr[:, px, :, py] = out.reshape(hx - 1, hy + 1, tz, LANES)

    def pointwise(i, _):
        g = gsr[i // 2, lax.rem(i, 2)].reshape(ey, tz, LANES)
        summed, grad = unit(pre[i], bias, xe[i + 1, 1 : 1 + ey], g, ch)
        at = pl.ds(pl.multiple_of(i * ey * tz, 16), ey * tz)
        s_ref[at] = summed.reshape(ey * tz, LANES).astype(BF16)
        gp_ref[at] = grad.reshape(ey * tz, LANES).astype(BF16)
        gp[i] = grad
        return 0

    lax.fori_loop(0, inner, pointwise, 0)
    gs_ref[...] = gsr[...].reshape(inner, ey, tz, LANES)[:, 1 : 1 + ty].reshape(
        inner * ty * tz, LANES
    )
    other = z_taps(gp[:, 1 : 1 + ty].reshape(inner * ty, tz, LANES))
    for a in range(3):
        wins = [
            with_ones(xe[a : a + inner, b + 1 : b + 1 + ty], a, b, ch)
            .reshape(inner * ty * tz, LANES)
            .astype(BF16)
            for b in range(3)
        ]
        acc_ref[a * 3 * LANES : (a + 1) * 3 * LANES] = lax.dot_general(
            jnp.concatenate(wins, axis=1), other, TN, preferred_element_type=F32
        )


def main_kernel(
    dims, x_ref, u_ref, core_ref, side_ref, near_ref, far_ref, wf, wd, bias, gpa_ref, sa_ref, acc_ref,
    send_ref, gpb_ref, sb_ref, gsb_ref, win_ref, other_ref,
    xe, ue, ss, pre, gsr, edge, pack,
):
    tx, ty, tz, ch = dims
    hx, hy = tx // 2, ty // 2
    ex, ey = tx + 2, ty + 2
    slab = ey * tz
    core = lax.axis_index("core")
    odd = lax.rem(lax.axis_index("gx"), 2)
    widen(dims, x_ref, u_ref, core_ref, side_ref, xe, ue, 2, 1)
    rows = 2 * (ty + 4) * tz
    inside = in_grid(1 - odd, "gx")
    for ref, low, real in ((near_ref, odd, True), (far_ref, 1 - odd, inside)):
        part = jnp.where(real, ref[...].astype(F32), 0.0)
        xe[pl.ds((1 - low) * (tx + 2), 2)] = part[:rows].reshape(2, ty + 4, tz, LANES)
        ue[pl.ds((1 - low) * (hx + 1), 1)] = part[rows:].reshape(1, hy + 2, tz, LANES)
    ss[1:hx] = sa_ref[...].astype(F32).reshape(hx - 1, 2, hy + 1, 2, tz, LANES)

    def edges(v, a, lower, upper):
        return jnp.concatenate([v[lower + a : lower + a + 2], v[upper + a : upper + a + 2]], axis=0)

    wins = [
        edges(xe, a, 0, ex - 2)[:, b : b + ey].reshape(4 * slab, LANES).astype(BF16)
        for a in range(3)
        for b in range(3)
    ]
    out = jnp.dot(jnp.concatenate(wins, axis=1), wf[...], preferred_element_type=F32)
    out = z_sum(out.reshape(4 * ey, tz, 3 * LANES), below, above)
    pre[...] = out.reshape(4, ey, tz, LANES)
    for px in (0, 1):
        for py in (0, 1):
            picks = []
            for a, sx in TERMS[px]:
                for b, sy in TERMS[py]:
                    win = jnp.concatenate(
                        [ue[sx, sy : sy + hy + 1], ue[hx + sx, sy : sy + hy + 1]], axis=0
                    )
                    picks.append((a, win, b))
            out = fine_gradient(2 * (hy + 1) * tz, wd, picks)
            out = z_sum(out.reshape(2 * (hy + 1), tz, 3 * LANES), above, below)
            gsr[:, px, :, py] = out.reshape(2, hy + 1, tz, LANES)
    for j, i in enumerate((0, 1, ex - 2, ex - 1)):
        g = gsr[j // 2, j % 2].reshape(ey, tz, LANES)
        summed, grad = unit(pre[j], bias, xe[i + 1, 1 : 1 + ey], g, ch)
        ss[i // 2, i % 2] = summed.reshape(hy + 1, 2, tz, LANES)
        sb_ref[j * slab : (j + 1) * slab] = summed.reshape(slab, LANES).astype(BF16)
        gpb_ref[j * slab : (j + 1) * slab] = grad.reshape(slab, LANES).astype(BF16)
        if j in (1, 2):
            edge[j - 1] = grad[1 : 1 + ty]
            gsb_ref[(j - 1) * ty * tz : j * ty * tz] = g[1 : 1 + ty].reshape(ty * tz, LANES)

    def fine_window(a, b):
        win = jnp.concatenate(
            [xe[a + 1, b + 1 : b + 1 + ty], xe[tx + a, b + 1 : b + 1 + ty]], axis=0
        )
        return with_ones(win, a, b, ch).reshape(2 * ty * tz, LANES).astype(BF16)

    def coarse_window(a, b):
        win = ss[a // 2 : a // 2 + hx, a % 2, b // 2 : b // 2 + hy, b % 2]
        return win.reshape(hx * hy * tz, LANES).astype(BF16)

    own = ue[1 : 1 + hx, 1 : 1 + hy].reshape(hx * hy, tz, LANES)
    for h, window, other in (
        (0, fine_window, z_taps(edge[...].reshape(2 * ty, tz, LANES))),
        (1, coarse_window, z_taps(own)),
    ):
        rows = other.shape[0]
        for ab in range(9):
            win_ref[h, :rows, ab * LANES : (ab + 1) * LANES] = window(ab // 3, ab % 3)
        other_ref[h, :rows] = other
        if rows < win_ref.shape[1]:
            win_ref[h, rows:] = jnp.zeros((win_ref.shape[1] - rows, win_ref.shape[2]), BF16)
            other_ref[h, rows:] = jnp.zeros((win_ref.shape[1] - rows, 3 * LANES), BF16)
    half_gradients(ch, 1 - core, win_ref, other_ref, acc_ref, pack)
    send_ref[...] = pack[...].astype(BF16)


def half_gradients(ch, h, win_ref, other_ref, acc_ref, pack):
    block_rows = ch * ch // LANES
    for a in range(3):
        part = slice(a * 3 * LANES, (a + 1) * 3 * LANES)
        out = lax.dot_general(win_ref[h, :, part], other_ref[h], TN, preferred_element_type=F32)
        out = out + jnp.where(h == 0, acc_ref[part], 0.0)
        for b in range(3):
            for e in range(3):
                at = (a * 9 + b * 3 + e) * block_rows
                block = out[b * LANES : b * LANES + ch, e * LANES : (e + 1) * LANES]
                pack[at : at + block_rows] = pack_block(block, ch)
        if a == 1:
            at = 27 * block_rows
            pack[at : at + 8] = out[LANES + ch : LANES + ch + 8, LANES : 2 * LANES]
    at = 27 * block_rows + 8
    pack[at:] = jnp.zeros((pack.shape[0] - at, LANES), F32)


def keep_kernel(ch, win_ref, other_ref, acc_ref, keep_ref):
    half_gradients(ch, lax.axis_index("core"), win_ref, other_ref, acc_ref, keep_ref)


def second_outputs(
    dims, x_ref, u_ref, gpa_ref, gpb_ref, gsa_ref, gsb_ref, sa_ref, sb_ref, wf, wd, down_ref, gv_ref,
    ge, ss, accd,
):
    tx, ty, tz, ch = dims
    hx, hy = tx // 2, ty // 2
    ex, ey = tx + 2, ty + 2
    slab = ey * tz
    ge[2:tx] = gpa_ref[...].astype(F32).reshape(tx - 2, ey, tz, LANES)
    ss[1:hx] = sa_ref[...].astype(F32).reshape(hx - 1, 2, hy + 1, 2, tz, LANES)
    for j, i in enumerate((0, 1, ex - 2, ex - 1)):
        ge[i] = gpb_ref[j * slab : (j + 1) * slab].astype(F32).reshape(ey, tz, LANES)
        ss[i // 2, i % 2] = (
            sb_ref[j * slab : (j + 1) * slab].astype(F32).reshape(hy + 1, 2, tz, LANES)
        )
    wins = [
        ss[a // 2 : a // 2 + hx, a % 2, b // 2 : b // 2 + hy, b % 2]
        .reshape(hx * hy * tz, LANES)
        .astype(BF16)
        for a in range(3)
        for b in range(3)
    ]
    out = jnp.dot(jnp.concatenate(wins, axis=1), wd[...], preferred_element_type=F32)
    out = z_sum(out.reshape(hx * hy, tz, 3 * LANES), below, above).reshape(hx * hy * tz, LANES)
    u = u_ref[...].astype(F32)
    accd[...] = out * jnp.broadcast_to(u[:, ch : ch + 1], u.shape)
    down_ref[...] = accd[pl.ds(0, hx * hy * tz // 2, stride=2), :][:, :ch].astype(BF16)

    wins = [
        ge[2 - a : 2 - a + tx, 2 - b : 2 - b + ty].reshape(tx * ty * tz, LANES).astype(BF16)
        for a in range(3)
        for b in range(3)
    ]
    taps = jnp.concatenate([wf[ab] for ab in range(9)], axis=1)
    out = lax.dot_general(jnp.concatenate(wins, axis=1), taps, NT, preferred_element_type=F32)
    out = z_sum(out.reshape(tx * ty, tz, 3 * LANES), above, below).reshape(tx * ty * tz, LANES)
    x = x_ref[...].astype(F32)
    live = jnp.broadcast_to(x[:, ch : ch + 1], x.shape)
    column = ty * tz
    grad = jnp.concatenate([gsb_ref[:column], gsa_ref[...], gsb_ref[column:]], axis=0)
    gv_ref[...] = ((grad + out) * live)[:, :ch].astype(BF16)


def peers_of(core):
    return 0, 1 + core, 2 - core, 3


def split_kernel(keep_ref, got_ref, own_ref, *to_refs):
    me = lax.rem(lax.axis_index("gx"), 2) * 2 + lax.rem(lax.axis_index("gyc"), 2)
    rows = own_ref.shape[0]
    for k, ref in zip(peers_of(lax.axis_index("core")), (own_ref, *to_refs)):
        at = pl.ds(pl.multiple_of((me ^ k) * rows, 16), rows)
        ref[...] = (keep_ref[at] + got_ref[at].astype(F32)).astype(ref.dtype)


def sum_kernel(own_ref, a_ref, b_ref, c_ref, out_ref):
    out_ref[...] = (
        own_ref[...] + a_ref[...].astype(F32) + b_ref[...].astype(F32) + c_ref[...].astype(F32)
    ).astype(BF16)


def unpacked_half(ch, factor, half, parts, full, out, bias):
    me = lax.rem(lax.axis_index("gx"), 2) * 2 + lax.rem(lax.axis_index("gyc"), 2)
    rows = parts[0].shape[0]
    block_rows = ch * ch // LANES
    for k, part in zip(peers_of(half), parts):
        at = pl.ds(pl.multiple_of((me ^ k) * rows, 16), rows)
        full[at] = part[...].astype(F32) * factor
    bias[...] = full[27 * block_rows + 1 : 27 * block_rows + 2]
    for t in range(27):
        out[t] = unpack_block(full[t * block_rows : (t + 1) * block_rows], ch)[:, :ch]
        yield t


def own_kernel(ch, factor, *refs):
    parts, (out, bias, full) = refs[:4], refs[4:]
    for _ in unpacked_half(ch, factor, lax.axis_index("core"), parts, full, out, bias):
        pass


def last_kernel(ch, factor, *refs):
    parts, (own, own_bias, conv_ref, down_ref, bias_ref, full, out, bias, bias_out, sems) = (
        refs[:4], refs[4:],
    )
    core = lax.axis_index("core")

    def moves(src, part, sem, first):
        for c, ref in ((0, conv_ref), (1, down_ref)):
            yield (core == c) == first, pltpu.make_async_copy(src.at[part], ref.at[part], sem)

    every = [(own, pl.ds(0, 27), sems.at[0], True)]
    every += [(out, pl.ds(a * 9, 9), sems.at[1 + a], False) for a in range(3)]

    def start(n):
        for wanted, copy in moves(*every[n]):
            pl.when(wanted)(copy.start)

    start(0)
    for t in unpacked_half(ch, factor, 1 - core, parts, full, out, bias):
        if t % 9 == 8:
            start(1 + t // 9)
    bias_out[...] = jnp.where(core == 0, own_bias[...], bias[...])[:, :ch]
    last = pltpu.make_async_copy(bias_out, bias_ref, sems.at[4])
    last.start()
    for move in every:
        for wanted, copy in moves(*move):
            pl.when(wanted)(copy.wait)
    last.wait()


def on_device(voxels, occupancy, conv_weight, conv_bias, down_weight, down_cotangent):
    tx, ty, tz, ch = voxels.shape
    hx, hy, hz = tx // 2, ty // 2, tz // 2
    ex, ey = tx + 2, ty + 2
    dims = (tx, ty, tz, ch)
    n_gx, n_gyc = lax.axis_size("gx"), lax.axis_size("gyc")
    fine, coarse = tx * ty * tz, hx * hy * tz

    side_rows = tx * 2 * tz + hx * tz
    row_rows = 2 * (ty + 4) * tz + (hy + 2) * tz
    x, u, to_core, to_side = call(
        functools.partial(first_kernel, dims),
        [((fine, LANES), BF16), ((coarse, LANES), BF16)] + [((side_rows, LANES), BF16)] * 2,
        (
            voxels.reshape(fine, ch),
            occupancy.reshape(tx * ty, tz),
            down_cotangent.reshape(hx * hy * hz, ch),
        ),
        [
            ((fine, LANES), F32),
            ((coarse, LANES), F32),
            ((fine, ch), BF16),
            ((tx * ty, tz), jnp.int32),
            ((hx * hy * hz, ch), BF16),
        ],
        vmem=4,
        far=(0, 1, 2),
        sems=3,
    )
    swap = [(0, 1), (1, 0)]
    n_gy = n_gyc * 2
    sides = [(i, (i + (1 if i % 2 else -1)) % n_gy) for i in range(n_gy)]
    from_core = lax.ppermute(to_core, "core", swap)
    from_side = lax.ppermute(to_side, ("gyc", "core"), sides)
    in_lanes, in_rows = ((9 * LANES, 3 * LANES), BF16), ((9, 3 * LANES, LANES), BF16)
    weights = call(
        functools.partial(weights_kernel, ch),
        [in_lanes, in_rows, ((1, LANES), F32), ((27, ch, ch), BF16), ((27, ch, ch), BF16)],
        (conv_weight, down_weight, conv_bias.reshape(1, ch)),
        [((1, ch), F32)],
        vmem=4,
        far=(0, 1, 2),
        sems=3,
    )
    from_core, from_side, *weights = lax.optimization_barrier((from_core, from_side, *weights))
    conv_lanes, down_rows, bias, raw_conv, raw_down = weights
    to_near, to_far = call(
        functools.partial(second_kernel, dims),
        [((row_rows, LANES), BF16)] * 2,
        (x, u, from_core, from_side),
        [((tx, ty + 4, tz, LANES), F32), ((hx, hy + 2, tz, LANES), F32)],
        vmem=4,
    )
    near = [(i, i ^ 1) for i in range(n_gx)]
    far = []
    for i in range(n_gx):
        peer = i + (1 if i % 2 else -1)
        for j in range(n_gy):
            to = i * n_gy + (j ^ 1) if peer in (-1, n_gx) else peer * n_gy + j
            far.append((i * n_gy + j, to))
    from_near = lax.ppermute(to_near, "gx", near)
    from_far = lax.ppermute(to_far, ("gx", "gyc", "core"), far)
    inner = tx - 2
    *results, = call(
        functools.partial(inner_kernel, dims),
        [((inner * ey * tz, LANES), BF16)] * 2
        + [((inner * ty * tz, LANES), F32), ((9 * LANES, 3 * LANES), F32)],
        (x, u, from_core, from_side, conv_lanes, down_rows, bias),
        [
            ((tx, ty + 4, tz, LANES), F32),
            ((hx, hy + 2, tz, LANES), F32),
            ((inner, ey, tz, LANES), F32),
            ((hx - 1, 2, hy + 1, 2, tz, LANES), F32),
            ((inner, ey, tz, LANES), F32),
        ],
        cost=pl.CostEstimate(flops=5_000_000_000, bytes_accessed=4_000_000, transcendentals=0),
        vmem=12,
    )
    from_far, from_near, *results = lax.optimization_barrier((from_far, from_near, *results))
    gp_inner, s_inner, gs_inner, acc = results

    block_rows = ch * ch // LANES
    half_rows = -(-(27 * block_rows + 8) // 64) * 64
    cells = max(2 * ty * tz, coarse)
    send, gp_edge, s_edge, gs_edge, wins, others = call(
        functools.partial(main_kernel, dims),
        [((half_rows, LANES), BF16)]
        + [((4 * ey * tz, LANES), BF16)] * 2
        + [((2 * ty * tz, LANES), F32)]
        + [((2, cells, 9 * LANES), BF16), ((2, cells, 3 * LANES), BF16)],
        (
            x, u, from_core, from_side, from_near, from_far, conv_lanes, down_rows, bias,
            gp_inner, s_inner, acc,
        ),
        [
            ((tx + 4, ty + 4, tz, LANES), F32),
            ((hx + 2, hy + 2, tz, LANES), F32),
            ((hx + 1, 2, hy + 1, 2, tz, LANES), F32),
            ((4, ey, tz, LANES), F32),
            ((2, 2, hy + 1, 2, tz, LANES), F32),
            ((2, ty, tz, LANES), F32),
            ((half_rows, LANES), F32),
        ],
        vmem=12,
    )
    got = lax.ppermute(send, "core", swap)
    (keep,) = call(
        functools.partial(keep_kernel, ch),
        [((half_rows, LANES), F32)],
        (wins, others, acc),
        cost=pl.CostEstimate(flops=2_000_000_000, bytes_accessed=4_000_000, transcendentals=0),
        vmem=6,
    )
    got, keep = lax.optimization_barrier((got, keep))

    rest = call(
        functools.partial(other_weights_kernel, ch),
        [in_rows, in_lanes],
        (raw_conv, raw_down),
        vmem=4,
    )
    conv_rows, down_lanes = rest
    down, grad_voxels = call(
        functools.partial(second_outputs, dims),
        [((hx * hy * hz, ch), BF16), ((fine, ch), BF16)],
        (x, u, gp_inner, gp_edge, gs_inner, gs_edge, s_inner, s_edge, conv_rows, down_lanes),
        [
            ((ex, ey, tz, LANES), F32),
            ((hx + 1, 2, hy + 1, 2, tz, LANES), F32),
            ((coarse, LANES), F32),
        ],
        cost=pl.CostEstimate(flops=5_000_000_000, bytes_accessed=4_000_000, transcendentals=0),
        vmem=12,
    )

    def plus(a, b):
        return (a.astype(F32) + b.astype(F32)).astype(BF16)

    quarter = half_rows // 4
    mine, *pieces = call(
        split_kernel,
        [((quarter, LANES), F32)] + [((quarter, LANES), BF16)] * 3,
        (keep, got),
        vmem=2,
    )

    def across(value, turn):
        route = []
        for i in range(n_gx):
            for j in range(n_gyc):
                for c in range(2):
                    k = peers_of(c)[turn]
                    peer = (i ^ (k >> 1)) * n_gyc + (j ^ (k & 1))
                    route.append(((i * n_gyc + j) * 2 + c, peer * 2 + c))
        return lax.ppermute(value, ("gx", "gyc", "core"), route)

    arrived = [across(piece, k) for k, piece in zip((1, 2, 3), pieces)]
    *arrived, down, grad_voxels = lax.optimization_barrier((*arrived, down, grad_voxels))
    (total,) = call(sum_kernel, [((quarter, LANES), BF16)], (mine, *arrived), vmem=2)
    steps = []
    for place, peers in ((0, n_gx), (1, n_gyc)):
        step = 2
        while step < peers:
            steps.append((step, 0) if place == 0 else (0, step))
            step *= 2
    for one, two in zip(steps, steps[::-1]):
        route = []
        for i in range(n_gx):
            for j in range(n_gyc):
                for c, (dx, dy) in enumerate((one, two)):
                    at = ((i * n_gyc + j) * 2 + c, ((i ^ dx) * n_gyc + (j ^ dy)) * 2 + c)
                    route.append(at)
        total = plus(total, lax.ppermute(total, ("gx", "gyc", "core"), route))
    own = [total] + [across(total, k) for k in (1, 2, 3)]
    other = []
    for piece in own:
        other.append(lax.ppermute(piece, "core", swap))
    factor = 1.0 / math.sqrt(tx * n_gx * ty * n_gy * tz)
    whole = [((27, ch, ch), F32), ((1, LANES), F32)]
    mine = call(
        functools.partial(own_kernel, ch, factor),
        whole,
        own,
        [((half_rows, LANES), F32)],
        cost=pl.CostEstimate(flops=1_000_000_000, bytes_accessed=4_000_000, transcendentals=0),
        vmem=4,
    )
    other[1], *mine = lax.optimization_barrier((other[1], *mine))
    grad_conv, grad_down, grad_bias = call(
        functools.partial(last_kernel, ch, factor),
        [((27, ch, ch), F32), ((27, ch, ch), F32), ((1, ch), F32)],
        (*other, *mine),
        [((half_rows, LANES), F32)] + whole + [((1, ch), F32)],
        vmem=8,
        far_outs=True,
        sems=5,
    )
    return (
        down.reshape(hx, hy, hz, ch),
        grad_voxels.reshape(tx, ty, tz, ch),
        grad_conv,
        grad_bias.reshape(ch),
        grad_down,
    )


def solution(mesh):
    n_gx, n_gy = mesh.shape["gx"], mesh.shape["gy"]
    split = Mesh(mesh.devices.reshape(n_gx, n_gy // 2, 2), ("gx", "gyc", "core"))
    gy = ("gyc", "core")
    placed = (
        P("gx", gy, None, None),
        P("gx", gy, None),
        P(),
        P(),
        P(),
        P("gx", gy, None, None),
    )

    return jax.shard_map(
        on_device,
        mesh=split,
        in_specs=placed,
        out_specs=(P("gx", gy, None, None), P("gx", gy, None, None), P(), P(), P()),
        check_vma=False,
    )
```

```python
import functools
import math

import jax
import jax.numpy as jnp
from jax import lax
from jax.experimental import pallas as pl
from jax.experimental.pallas import tpu as pltpu
from jax.sharding import Mesh
from jax.sharding import PartitionSpec as P


LANES = 128
F32 = jnp.float32
BF16 = jnp.bfloat16
NT = (((1,), (1,)), ((), ()))
TN = (((0,), (0,)), ((), ()))
MIB = 1024 * 1024


def call(body, outs, args, scratch=(), cost=None, vmem=8, far=(), far_outs=False, sems=0):
    near_spec = pl.BlockSpec(memory_space=pltpu.VMEM)
    far_spec = pl.BlockSpec(memory_space=pltpu.HBM)
    args = [
        pltpu.with_memory_space_constraint(a, pltpu.HBM) if i in far else a
        for i, a in enumerate(args)
    ]
    return pl.pallas_call(
        body,
        out_shape=tuple(jax.ShapeDtypeStruct(s, d) for s, d in outs),
        in_specs=[far_spec if i in far else near_spec for i in range(len(args))],
        out_specs=tuple(far_spec if far_outs else near_spec for _ in outs),
        scratch_shapes=[pltpu.VMEM(s, d) for s, d in scratch]
        + ([pltpu.SemaphoreType.DMA((sems,))] if sems else []),
        compiler_params=pltpu.CompilerParams(vmem_limit_bytes=vmem * MIB),
        cost_estimate=cost,
    )(*args)


def fetch(pairs, sems):
    copies = [pltpu.make_async_copy(a, b, sems.at[i]) for i, (a, b) in enumerate(pairs)]
    for copy in copies:
        copy.start()
    for copy in copies:
        copy.wait()


def lane_of(shape):
    return lax.broadcasted_iota(jnp.int32, shape, len(shape) - 1)


def z_of(shape):
    return lax.broadcasted_iota(jnp.int32, shape, len(shape) - 2)


def below(v):
    return jnp.where(z_of(v.shape) == 0, 0.0, pltpu.roll(v, 1, axis=1))


def above(v):
    top = v.shape[1] - 1
    return jnp.where(z_of(v.shape) == top, 0.0, pltpu.roll(v, top, axis=1))


def first_kernel(
    dims, vox_far, occ_far, cot_far, x_ref, u_ref, core_ref, side_ref,
    xs, us, vox_ref, occ_ref, cot_ref, sems,
):
    tx, ty, tz, ch = dims
    fetch(((vox_far, vox_ref), (occ_far, occ_ref), (cot_far, cot_ref)), sems)
    hx, hy = tx // 2, ty // 2
    occ = jnp.broadcast_to(occ_ref[...].astype(F32)[:, :, None], (tx * ty, tz, LANES))
    xs[...] = jnp.zeros(xs.shape, F32)
    xs[:, :ch] = vox_ref[...].astype(F32)
    x = xs[...].reshape(tx * ty, tz, LANES)
    x = jnp.where(lane_of(x.shape) == ch, 1.0, x) * occ
    xs[...] = x.reshape(xs.shape)
    x_ref[...] = xs[...].astype(BF16)
    pairs = occ.reshape(hx, 2, hy, 2, tz, LANES)
    pairs = jnp.maximum(pairs[:, 0], pairs[:, 1])
    pairs = jnp.maximum(pairs[:, :, 0], pairs[:, :, 1]).reshape(hx * hy, tz, LANES)
    coarse = jnp.maximum(pairs, pltpu.roll(pairs, tz - 1, axis=1))
    us[...] = jnp.zeros(us.shape, F32)
    cot = jnp.concatenate(
        [cot_ref[...].astype(F32), jnp.zeros((hx * hy * tz // 2, LANES - ch), F32)], axis=1
    )
    us[pl.ds(0, hx * hy * tz // 2, stride=2), :] = cot
    u = us[...].reshape(hx * hy, tz, LANES)
    even = lax.rem(z_of(u.shape), 2) == 0
    u = jnp.where((lane_of(u.shape) == ch) & even, 1.0, u) * coarse
    us[...] = u.reshape(us.shape)
    u_ref[...] = us[...].astype(BF16)
    core = lax.axis_index("core")
    x4, u4 = xs.reshape(tx, ty, tz, LANES), us.reshape(hx, hy, tz, LANES)
    rows = tx * 2 * tz
    for ref, low in ((core_ref, core), (side_ref, 1 - core)):
        start = (1 - low) * (ty - 2)
        ref[:rows] = x4[:, pl.ds(start, 2)].reshape(rows, LANES).astype(BF16)
        ref[rows:] = (
            u4[:, pl.ds((1 - low) * (hy - 1), 1)].reshape(hx * tz, LANES).astype(BF16)
        )


def second_kernel(dims, x_ref, u_ref, core_ref, side_ref, near_ref, far_ref, xe, ue):
    tx, ty, tz, _ = dims
    widen(dims, x_ref, u_ref, core_ref, side_ref, xe, ue, 0, 0)
    odd = lax.rem(lax.axis_index("gx"), 2)
    rows = 2 * (ty + 4) * tz
    hx, hy = tx // 2, ty // 2
    for ref, low in ((near_ref, odd), (far_ref, 1 - odd)):
        ref[:rows] = xe[pl.ds((1 - low) * (tx - 2), 2)].reshape(rows, LANES).astype(BF16)
        ref[rows:] = (
            ue[pl.ds((1 - low) * (hx - 1), 1)].reshape((hy + 2) * tz, LANES).astype(BF16)
        )


def widen(dims, x_ref, u_ref, core_ref, side_ref, xe, ue, x0, u0):
    tx, ty, tz, _ = dims
    hx, hy = tx // 2, ty // 2
    rows = tx * 2 * tz
    core = lax.axis_index("core")
    xe[x0 : x0 + tx, 2 : 2 + ty] = x_ref[...].astype(F32).reshape(tx, ty, tz, LANES)
    ue[u0 : u0 + hx, 1 : 1 + hy] = u_ref[...].astype(F32).reshape(hx, hy, tz, LANES)
    inside = in_grid(1 - core, "gyc")
    for ref, low, real in ((core_ref, core, True), (side_ref, 1 - core, inside)):
        part = jnp.where(real, ref[...].astype(F32), 0.0)
        xe[x0 : x0 + tx, pl.ds((1 - low) * (ty + 2), 2)] = part[:rows].reshape(tx, 2, tz, LANES)
        ue[u0 : u0 + hx, pl.ds((1 - low) * (hy + 1), 1)] = part[rows:].reshape(hx, 1, tz, LANES)


def in_grid(low, axis):
    me = lax.axis_index(axis)
    return jnp.where(low == 1, me > 0, me < lax.axis_size(axis) - 1)


def taps_in_rows(ch, w_ref, out):
    out[...] = jnp.zeros(out.shape, BF16)
    for t in range(w_ref.shape[0]):
        out[t // 3, (t % 3) * LANES : (t % 3) * LANES + ch, :ch] = w_ref[t]


def taps_in_lanes(ch, w_ref, out):
    out[...] = jnp.zeros(out.shape, BF16)
    for t in range(w_ref.shape[0]):
        at, lane = t // 3 * LANES, t % 3 * LANES
        out[at : at + ch, lane : lane + ch] = w_ref[t]


def weights_kernel(ch, cw_far, dw_far, bias_far, cl_ref, dr_ref, b_ref, cw, dw, bias, sems):
    fetch(((cw_far, cw), (dw_far, dw), (bias_far, bias)), sems)
    taps_in_lanes(ch, cw, cl_ref)
    taps_in_rows(ch, dw, dr_ref)
    b_ref[...] = jnp.zeros(b_ref.shape, F32)
    b_ref[:, :ch] = bias[...]


def other_weights_kernel(ch, cw, dw, cr_ref, dl_ref):
    taps_in_rows(ch, cw, cr_ref)
    taps_in_lanes(ch, dw, dl_ref)


def three(v):
    return v[:, :, :LANES], v[:, :, LANES : 2 * LANES], v[:, :, 2 * LANES :]


def pack_block(block, ch):
    free = LANES - ch
    keep = ch * ch // LANES
    tail = block[keep:ch]
    parts = [
        pltpu.roll(tail, (LANES - free - p * free) % LANES, axis=1) for p in range(ch // free)
    ]
    parts = jnp.concatenate(parts, axis=0)
    main = block[:keep]
    return jnp.where(lane_of(main.shape) < ch, main, parts)


def unpack_block(packed, ch):
    free = LANES - ch
    keep = ch * ch // LANES
    tall = ch - keep
    lane = lane_of((tall, LANES))
    tail = None
    for p in range(ch // free):
        part = packed[p * tall : (p + 1) * tall]
        part = pltpu.roll(part, (free + p * free) % LANES, axis=1)
        tail = part if tail is None else jnp.where(lane < p * free, tail, part)
    return jnp.concatenate([packed, tail], axis=0)


def fine_gradient(rows, wd, picks):
    wins = [win.reshape(rows, LANES).astype(BF16) for _, win, _ in picks]
    taps = [wd[a * 3 + b] for a, _, b in picks]
    return lax.dot_general(
        jnp.concatenate(wins, axis=1), jnp.concatenate(taps, axis=1), NT,
        preferred_element_type=F32,
    )


def z_sum(out, lower, upper):
    low, same, high = three(out)
    return lower(low) + same + upper(high)


def unit(v, bias, x, g, ch):
    v = v + bias[...].reshape(1, 1, LANES)
    live = jnp.broadcast_to(x[:, :, ch : ch + 1], x.shape)
    s = 1.0 / (1.0 + jnp.exp(-v))
    summed = (x + live * (v * s)).astype(BF16).astype(F32)
    grad = (g * live * s * (1.0 + v * (1.0 - s))).astype(BF16).astype(F32)
    return summed, grad


def with_ones(win, a, b, ch):
    if a == 1 and b == 1:
        win = jnp.where(lane_of(win.shape) == ch + 1, 1.0, win)
    return win


def z_taps(other):
    cells = other.shape[0] * other.shape[1]
    other = jnp.concatenate([above(other), other, below(other)], axis=2)
    return other.reshape(cells, 3 * LANES).astype(BF16)


TERMS = {0: ((2, 0), (0, 1)), 1: ((1, 1),)}


def inner_kernel(
    dims, x_ref, u_ref, core_ref, side_ref, wf, wd, bias, gp_ref, s_ref, gs_ref, acc_ref,
    xe, ue, pre, gsr, gp,
):
    tx, ty, tz, ch = dims
    hx, hy = tx // 2, ty // 2
    ey, inner = ty + 2, tx - 2
    widen(dims, x_ref, u_ref, core_ref, side_ref, xe, ue, 0, 0)
    wins = [
        xe[a : a + inner, b : b + ey].reshape(inner * ey * tz, LANES).astype(BF16)
        for a in range(3)
        for b in range(3)
    ]
    out = jnp.dot(jnp.concatenate(wins, axis=1), wf[...], preferred_element_type=F32)
    out = z_sum(out.reshape(inner * ey, tz, 3 * LANES), below, above)
    pre[...] = out.reshape(inner, ey, tz, LANES)
    for px in (0, 1):
        for py in (0, 1):
            picks = [
                (a, ue[sx : sx + hx - 1, sy : sy + hy + 1], b)
                for a, sx in TERMS[px]
                for b, sy in TERMS[py]
            ]
            out = fine_gradient((hx - 1) * (hy + 1) * tz, wd, picks)
            out = z_sum(out.reshape((hx - 1) * (hy + 1), tz, 3 * LANES), above, below)
            gsr[:, px, :, py] = out.reshape(hx - 1, hy + 1, tz, LANES)

    def pointwise(i, _):
        g = gsr[i // 2, lax.rem(i, 2)].reshape(ey, tz, LANES)
        summed, grad = unit(pre[i], bias, xe[i + 1, 1 : 1 + ey], g, ch)
        at = pl.ds(pl.multiple_of(i * ey * tz, 16), ey * tz)
        s_ref[at] = summed.reshape(ey * tz, LANES).astype(BF16)
        gp_ref[at] = grad.reshape(ey * tz, LANES).astype(BF16)
        gp[i] = grad
        return 0

    lax.fori_loop(0, inner, pointwise, 0)
    gs_ref[...] = gsr[...].reshape(inner, ey, tz, LANES)[:, 1 : 1 + ty].reshape(
        inner * ty * tz, LANES
    )
    other = z_taps(gp[:, 1 : 1 + ty].reshape(inner * ty, tz, LANES))
    for a in range(3):
        wins = [
            with_ones(xe[a : a + inner, b + 1 : b + 1 + ty], a, b, ch)
            .reshape(inner * ty * tz, LANES)
            .astype(BF16)
            for b in range(3)
        ]
        acc_ref[a * 3 * LANES : (a + 1) * 3 * LANES] = lax.dot_general(
            jnp.concatenate(wins, axis=1), other, TN, preferred_element_type=F32
        )


def main_kernel(
    dims, x_ref, u_ref, core_ref, side_ref, near_ref, far_ref, wf, wd, bias, gpa_ref, sa_ref, acc_ref,
    send_ref, gpb_ref, sb_ref, gsb_ref, win_ref, other_ref,
    xe, ue, ss, pre, gsr, edge, pack,
):
    tx, ty, tz, ch = dims
    hx, hy = tx // 2, ty // 2
    ex, ey = tx + 2, ty + 2
    slab = ey * tz
    core = lax.axis_index("core")
    odd = lax.rem(lax.axis_index("gx"), 2)
    widen(dims, x_ref, u_ref, core_ref, side_ref, xe, ue, 2, 1)
    rows = 2 * (ty + 4) * tz
    inside = in_grid(1 - odd, "gx")
    for ref, low, real in ((near_ref, odd, True), (far_ref, 1 - odd, inside)):
        part = jnp.where(real, ref[...].astype(F32), 0.0)
        xe[pl.ds((1 - low) * (tx + 2), 2)] = part[:rows].reshape(2, ty + 4, tz, LANES)
        ue[pl.ds((1 - low) * (hx + 1), 1)] = part[rows:].reshape(1, hy + 2, tz, LANES)
    ss[1:hx] = sa_ref[...].astype(F32).reshape(hx - 1, 2, hy + 1, 2, tz, LANES)

    def edges(v, a, lower, upper):
        return jnp.concatenate([v[lower + a : lower + a + 2], v[upper + a : upper + a + 2]], axis=0)

    wins = [
        edges(xe, a, 0, ex - 2)[:, b : b + ey].reshape(4 * slab, LANES).astype(BF16)
        for a in range(3)
        for b in range(3)
    ]
    out = jnp.dot(jnp.concatenate(wins, axis=1), wf[...], preferred_element_type=F32)
    out = z_sum(out.reshape(4 * ey, tz, 3 * LANES), below, above)
    pre[...] = out.reshape(4, ey, tz, LANES)
    for px in (0, 1):
        for py in (0, 1):
            picks = []
            for a, sx in TERMS[px]:
                for b, sy in TERMS[py]:
                    win = jnp.concatenate(
                        [ue[sx, sy : sy + hy + 1], ue[hx + sx, sy : sy + hy + 1]], axis=0
                    )
                    picks.append((a, win, b))
            out = fine_gradient(2 * (hy + 1) * tz, wd, picks)
            out = z_sum(out.reshape(2 * (hy + 1), tz, 3 * LANES), above, below)
            gsr[:, px, :, py] = out.reshape(2, hy + 1, tz, LANES)
    for j, i in enumerate((0, 1, ex - 2, ex - 1)):
        g = gsr[j // 2, j % 2].reshape(ey, tz, LANES)
        summed, grad = unit(pre[j], bias, xe[i + 1, 1 : 1 + ey], g, ch)
        ss[i // 2, i % 2] = summed.reshape(hy + 1, 2, tz, LANES)
        sb_ref[j * slab : (j + 1) * slab] = summed.reshape(slab, LANES).astype(BF16)
        gpb_ref[j * slab : (j + 1) * slab] = grad.reshape(slab, LANES).astype(BF16)
        if j in (1, 2):
            edge[j - 1] = grad[1 : 1 + ty]
            gsb_ref[(j - 1) * ty * tz : j * ty * tz] = g[1 : 1 + ty].reshape(ty * tz, LANES)

    def fine_window(a, b):
        win = jnp.concatenate(
            [xe[a + 1, b + 1 : b + 1 + ty], xe[tx + a, b + 1 : b + 1 + ty]], axis=0
        )
        return with_ones(win, a, b, ch).reshape(2 * ty * tz, LANES).astype(BF16)

    def coarse_window(a, b):
        win = ss[a // 2 : a // 2 + hx, a % 2, b // 2 : b // 2 + hy, b % 2]
        return win.reshape(hx * hy * tz, LANES).astype(BF16)

    own = ue[1 : 1 + hx, 1 : 1 + hy].reshape(hx * hy, tz, LANES)
    for h, window, other in (
        (0, fine_window, z_taps(edge[...].reshape(2 * ty, tz, LANES))),
        (1, coarse_window, z_taps(own)),
    ):
        rows = other.shape[0]
        for ab in range(9):
            win_ref[h, :rows, ab * LANES : (ab + 1) * LANES] = window(ab // 3, ab % 3)
        other_ref[h, :rows] = other
        if rows < win_ref.shape[1]:
            win_ref[h, rows:] = jnp.zeros((win_ref.shape[1] - rows, win_ref.shape[2]), BF16)
            other_ref[h, rows:] = jnp.zeros((win_ref.shape[1] - rows, 3 * LANES), BF16)
    half_gradients(ch, 1 - core, win_ref, other_ref, acc_ref, pack)
    send_ref[...] = pack[...].astype(BF16)


def half_gradients(ch, h, win_ref, other_ref, acc_ref, pack):
    block_rows = ch * ch // LANES
    for a in range(3):
        part = slice(a * 3 * LANES, (a + 1) * 3 * LANES)
        out = lax.dot_general(win_ref[h, :, part], other_ref[h], TN, preferred_element_type=F32)
        out = out + jnp.where(h == 0, acc_ref[part], 0.0)
        for b in range(3):
            for e in range(3):
                at = (a * 9 + b * 3 + e) * block_rows
                block = out[b * LANES : b * LANES + ch, e * LANES : (e + 1) * LANES]
                pack[at : at + block_rows] = pack_block(block, ch)
        if a == 1:
            at = 27 * block_rows
            pack[at : at + 8] = out[LANES + ch : LANES + ch + 8, LANES : 2 * LANES]
    at = 27 * block_rows + 8
    pack[at:] = jnp.zeros((pack.shape[0] - at, LANES), F32)


def keep_kernel(ch, win_ref, other_ref, acc_ref, keep_ref):
    half_gradients(ch, lax.axis_index("core"), win_ref, other_ref, acc_ref, keep_ref)


def second_outputs(
    dims, x_ref, u_ref, gpa_ref, gpb_ref, gsa_ref, gsb_ref, sa_ref, sb_ref, wf, wd, down_ref, gv_ref,
    ge, ss, accd,
):
    tx, ty, tz, ch = dims
    hx, hy = tx // 2, ty // 2
    ex, ey = tx + 2, ty + 2
    slab = ey * tz
    ge[2:tx] = gpa_ref[...].astype(F32).reshape(tx - 2, ey, tz, LANES)
    ss[1:hx] = sa_ref[...].astype(F32).reshape(hx - 1, 2, hy + 1, 2, tz, LANES)
    for j, i in enumerate((0, 1, ex - 2, ex - 1)):
        ge[i] = gpb_ref[j * slab : (j + 1) * slab].astype(F32).reshape(ey, tz, LANES)
        ss[i // 2, i % 2] = (
            sb_ref[j * slab : (j + 1) * slab].astype(F32).reshape(hy + 1, 2, tz, LANES)
        )
    wins = [
        ss[a // 2 : a // 2 + hx, a % 2, b // 2 : b // 2 + hy, b % 2]
        .reshape(hx * hy * tz, LANES)
        .astype(BF16)
        for a in range(3)
        for b in range(3)
    ]
    out = jnp.dot(jnp.concatenate(wins, axis=1), wd[...], preferred_element_type=F32)
    out = z_sum(out.reshape(hx * hy, tz, 3 * LANES), below, above).reshape(hx * hy * tz, LANES)
    u = u_ref[...].astype(F32)
    accd[...] = out * jnp.broadcast_to(u[:, ch : ch + 1], u.shape)
    down_ref[...] = accd[pl.ds(0, hx * hy * tz // 2, stride=2), :][:, :ch].astype(BF16)

    wins = [
        ge[2 - a : 2 - a + tx, 2 - b : 2 - b + ty].reshape(tx * ty * tz, LANES).astype(BF16)
        for a in range(3)
        for b in range(3)
    ]
    taps = jnp.concatenate([wf[ab] for ab in range(9)], axis=1)
    out = lax.dot_general(jnp.concatenate(wins, axis=1), taps, NT, preferred_element_type=F32)
    out = z_sum(out.reshape(tx * ty, tz, 3 * LANES), above, below).reshape(tx * ty * tz, LANES)
    x = x_ref[...].astype(F32)
    live = jnp.broadcast_to(x[:, ch : ch + 1], x.shape)
    column = ty * tz
    grad = jnp.concatenate([gsb_ref[:column], gsa_ref[...], gsb_ref[column:]], axis=0)
    gv_ref[...] = ((grad + out) * live)[:, :ch].astype(BF16)


def peers_of(core):
    return 0, 1 + core, 2 - core, 3


def split_kernel(keep_ref, got_ref, own_ref, *to_refs):
    me = lax.rem(lax.axis_index("gx"), 2) * 2 + lax.rem(lax.axis_index("gyc"), 2)
    rows = own_ref.shape[0]
    for k, ref in zip(peers_of(lax.axis_index("core")), (own_ref, *to_refs)):
        at = pl.ds(pl.multiple_of((me ^ k) * rows, 16), rows)
        ref[...] = (keep_ref[at] + got_ref[at].astype(F32)).astype(ref.dtype)


def sum_kernel(own_ref, a_ref, b_ref, c_ref, out_ref):
    out_ref[...] = (
        own_ref[...] + a_ref[...].astype(F32) + b_ref[...].astype(F32) + c_ref[...].astype(F32)
    ).astype(BF16)


def unpacked_half(ch, factor, half, parts, full, out, bias):
    me = lax.rem(lax.axis_index("gx"), 2) * 2 + lax.rem(lax.axis_index("gyc"), 2)
    rows = parts[0].shape[0]
    block_rows = ch * ch // LANES
    for k, part in zip(peers_of(half), parts):
        at = pl.ds(pl.multiple_of((me ^ k) * rows, 16), rows)
        full[at] = part[...].astype(F32) * factor
    bias[...] = full[27 * block_rows + 1 : 27 * block_rows + 2]
    for t in range(27):
        out[t] = unpack_block(full[t * block_rows : (t + 1) * block_rows], ch)[:, :ch]
        yield t


def own_kernel(ch, factor, *refs):
    parts, (out, bias, full) = refs[:4], refs[4:]
    for _ in unpacked_half(ch, factor, lax.axis_index("core"), parts, full, out, bias):
        pass


def last_kernel(ch, factor, *refs):
    parts, (own, own_bias, conv_ref, down_ref, bias_ref, full, out, bias, bias_out, sems) = (
        refs[:4], refs[4:],
    )
    core = lax.axis_index("core")

    def moves(src, part, sem, first):
        for c, ref in ((0, conv_ref), (1, down_ref)):
            yield (core == c) == first, pltpu.make_async_copy(src.at[part], ref.at[part], sem)

    every = [(own, pl.ds(0, 27), sems.at[0], True)]
    every += [(out, pl.ds(a * 9, 9), sems.at[1 + a], False) for a in range(3)]

    def start(n):
        for wanted, copy in moves(*every[n]):
            pl.when(wanted)(copy.start)

    start(0)
    for t in unpacked_half(ch, factor, 1 - core, parts, full, out, bias):
        if t % 9 == 8:
            start(1 + t // 9)
    bias_out[...] = jnp.where(core == 0, own_bias[...], bias[...])[:, :ch]
    last = pltpu.make_async_copy(bias_out, bias_ref, sems.at[4])
    last.start()
    for move in every:
        for wanted, copy in moves(*move):
            pl.when(wanted)(copy.wait)
    last.wait()


def on_device(voxels, occupancy, conv_weight, conv_bias, down_weight, down_cotangent):
    tx, ty, tz, ch = voxels.shape
    hx, hy, hz = tx // 2, ty // 2, tz // 2
    ex, ey = tx + 2, ty + 2
    dims = (tx, ty, tz, ch)
    n_gx, n_gyc = lax.axis_size("gx"), lax.axis_size("gyc")
    fine, coarse = tx * ty * tz, hx * hy * tz

    side_rows = tx * 2 * tz + hx * tz
    row_rows = 2 * (ty + 4) * tz + (hy + 2) * tz
    x, u, to_core, to_side = call(
        functools.partial(first_kernel, dims),
        [((fine, LANES), BF16), ((coarse, LANES), BF16)] + [((side_rows, LANES), BF16)] * 2,
        (
            voxels.reshape(fine, ch),
            occupancy.reshape(tx * ty, tz),
            down_cotangent.reshape(hx * hy * hz, ch),
        ),
        [
            ((fine, LANES), F32),
            ((coarse, LANES), F32),
            ((fine, ch), BF16),
            ((tx * ty, tz), jnp.int32),
            ((hx * hy * hz, ch), BF16),
        ],
        vmem=4,
        far=(0, 1, 2),
        sems=3,
    )
    swap = [(0, 1), (1, 0)]
    n_gy = n_gyc * 2
    sides = []
    for i in range(n_gx):
        for j in range(n_gy):
            peer = j + (1 if j % 2 else -1)
            to = (i ^ 1) * n_gy + j if peer in (-1, n_gy) else i * n_gy + peer
            sides.append((i * n_gy + j, to))
    from_core = lax.ppermute(to_core, "core", swap)
    from_side = lax.ppermute(to_side, ("gx", "gyc", "core"), sides)
    in_lanes, in_rows = ((9 * LANES, 3 * LANES), BF16), ((9, 3 * LANES, LANES), BF16)
    weights = call(
        functools.partial(weights_kernel, ch),
        [in_lanes, in_rows, ((1, LANES), F32), ((27, ch, ch), BF16), ((27, ch, ch), BF16)],
        (conv_weight, down_weight, conv_bias.reshape(1, ch)),
        [((1, ch), F32)],
        vmem=4,
        far=(0, 1, 2),
        sems=3,
    )
    from_core, from_side, *weights = lax.optimization_barrier((from_core, from_side, *weights))
    conv_lanes, down_rows, bias, raw_conv, raw_down = weights
    to_near, to_far = call(
        functools.partial(second_kernel, dims),
        [((row_rows, LANES), BF16)] * 2,
        (x, u, from_core, from_side),
        [((tx, ty + 4, tz, LANES), F32), ((hx, hy + 2, tz, LANES), F32)],
        vmem=4,
    )
    near = [(i, i ^ 1) for i in range(n_gx)]
    far = []
    for i in range(n_gx):
        peer = i + (1 if i % 2 else -1)
        for j in range(n_gy):
            to = i * n_gy + (j ^ 1) if peer in (-1, n_gx) else peer * n_gy + j
            far.append((i * n_gy + j, to))
    from_near = lax.ppermute(to_near, "gx", near)
    from_far = lax.ppermute(to_far, ("gx", "gyc", "core"), far)
    inner = tx - 2
    *results, = call(
        functools.partial(inner_kernel, dims),
        [((inner * ey * tz, LANES), BF16)] * 2
        + [((inner * ty * tz, LANES), F32), ((9 * LANES, 3 * LANES), F32)],
        (x, u, from_core, from_side, conv_lanes, down_rows, bias),
        [
            ((tx, ty + 4, tz, LANES), F32),
            ((hx, hy + 2, tz, LANES), F32),
            ((inner, ey, tz, LANES), F32),
            ((hx - 1, 2, hy + 1, 2, tz, LANES), F32),
            ((inner, ey, tz, LANES), F32),
        ],
        cost=pl.CostEstimate(flops=5_000_000_000, bytes_accessed=4_000_000, transcendentals=0),
        vmem=12,
    )
    from_far, from_near, *results = lax.optimization_barrier((from_far, from_near, *results))
    gp_inner, s_inner, gs_inner, acc = results

    block_rows = ch * ch // LANES
    half_rows = -(-(27 * block_rows + 8) // 64) * 64
    cells = max(2 * ty * tz, coarse)
    send, gp_edge, s_edge, gs_edge, wins, others = call(
        functools.partial(main_kernel, dims),
        [((half_rows, LANES), BF16)]
        + [((4 * ey * tz, LANES), BF16)] * 2
        + [((2 * ty * tz, LANES), F32)]
        + [((2, cells, 9 * LANES), BF16), ((2, cells, 3 * LANES), BF16)],
        (
            x, u, from_core, from_side, from_near, from_far, conv_lanes, down_rows, bias,
            gp_inner, s_inner, acc,
        ),
        [
            ((tx + 4, ty + 4, tz, LANES), F32),
            ((hx + 2, hy + 2, tz, LANES), F32),
            ((hx + 1, 2, hy + 1, 2, tz, LANES), F32),
            ((4, ey, tz, LANES), F32),
            ((2, 2, hy + 1, 2, tz, LANES), F32),
            ((2, ty, tz, LANES), F32),
            ((half_rows, LANES), F32),
        ],
        vmem=12,
    )
    got = lax.ppermute(send, "core", swap)
    (keep,) = call(
        functools.partial(keep_kernel, ch),
        [((half_rows, LANES), F32)],
        (wins, others, acc),
        cost=pl.CostEstimate(flops=2_000_000_000, bytes_accessed=4_000_000, transcendentals=0),
        vmem=6,
    )
    got, keep = lax.optimization_barrier((got, keep))

    rest = call(
        functools.partial(other_weights_kernel, ch),
        [in_rows, in_lanes],
        (raw_conv, raw_down),
        vmem=4,
    )
    conv_rows, down_lanes = rest
    down, grad_voxels = call(
        functools.partial(second_outputs, dims),
        [((hx * hy * hz, ch), BF16), ((fine, ch), BF16)],
        (x, u, gp_inner, gp_edge, gs_inner, gs_edge, s_inner, s_edge, conv_rows, down_lanes),
        [
            ((ex, ey, tz, LANES), F32),
            ((hx + 1, 2, hy + 1, 2, tz, LANES), F32),
            ((coarse, LANES), F32),
        ],
        cost=pl.CostEstimate(flops=5_000_000_000, bytes_accessed=4_000_000, transcendentals=0),
        vmem=12,
    )

    def plus(a, b):
        return (a.astype(F32) + b.astype(F32)).astype(BF16)

    quarter = half_rows // 4
    mine, *pieces = call(
        split_kernel,
        [((quarter, LANES), F32)] + [((quarter, LANES), BF16)] * 3,
        (keep, got),
        vmem=2,
    )

    def across(value, turn):
        route = []
        for i in range(n_gx):
            for j in range(n_gyc):
                for c in range(2):
                    k = peers_of(c)[turn]
                    peer = (i ^ (k >> 1)) * n_gyc + (j ^ (k & 1))
                    route.append(((i * n_gyc + j) * 2 + c, peer * 2 + c))
        return lax.ppermute(value, ("gx", "gyc", "core"), route)

    arrived = [across(piece, k) for k, piece in zip((1, 2, 3), pieces)]
    *arrived, down, grad_voxels = lax.optimization_barrier((*arrived, down, grad_voxels))
    (total,) = call(sum_kernel, [((quarter, LANES), BF16)], (mine, *arrived), vmem=2)
    steps = []
    for place, peers in ((0, n_gx), (1, n_gyc)):
        step = 2
        while step < peers:
            steps.append((step, 0) if place == 0 else (0, step))
            step *= 2
    for one, two in zip(steps, steps[::-1]):
        route = []
        for i in range(n_gx):
            for j in range(n_gyc):
                for c, (dx, dy) in enumerate((one, two)):
                    at = ((i * n_gyc + j) * 2 + c, ((i ^ dx) * n_gyc + (j ^ dy)) * 2 + c)
                    route.append(at)
        total = plus(total, lax.ppermute(total, ("gx", "gyc", "core"), route))
    own = [total] + [across(total, k) for k in (1, 2, 3)]
    other = []
    for piece in own:
        other.append(lax.ppermute(piece, "core", swap))
    factor = 1.0 / math.sqrt(tx * n_gx * ty * n_gy * tz)
    whole = [((27, ch, ch), F32), ((1, LANES), F32)]
    mine = call(
        functools.partial(own_kernel, ch, factor),
        whole,
        own,
        [((half_rows, LANES), F32)],
        cost=pl.CostEstimate(flops=1_000_000_000, bytes_accessed=4_000_000, transcendentals=0),
        vmem=4,
    )
    other[1], *mine = lax.optimization_barrier((other[1], *mine))
    grad_conv, grad_down, grad_bias = call(
        functools.partial(last_kernel, ch, factor),
        [((27, ch, ch), F32), ((27, ch, ch), F32), ((1, ch), F32)],
        (*other, *mine),
        [((half_rows, LANES), F32)] + whole + [((1, ch), F32)],
        vmem=8,
        far_outs=True,
        sems=5,
    )
    return (
        down.reshape(hx, hy, hz, ch),
        grad_voxels.reshape(tx, ty, tz, ch),
        grad_conv,
        grad_bias.reshape(ch),
        grad_down,
    )


def solution(mesh):
    n_gx, n_gy = mesh.shape["gx"], mesh.shape["gy"]
    split = Mesh(mesh.devices.reshape(n_gx, n_gy // 2, 2), ("gx", "gyc", "core"))
    gy = ("gyc", "core")
    placed = (
        P("gx", gy, None, None),
        P("gx", gy, None),
        P(),
        P(),
        P(),
        P("gx", gy, None, None),
    )

    return jax.shard_map(
        on_device,
        mesh=split,
        in_specs=placed,
        out_specs=(P("gx", gy, None, None), P("gx", gy, None, None), P(), P(), P()),
        check_vma=False,
    )
```
